128 devices in a mesh: rows: 32 (over x, y, z_lo), feat: 4 (over z_hi, core).
Axes of the slice: x: 4, y: 4, z: 4 (z_hi: 2, z_lo: 2; z = z_hi * 2 + z_lo), core: 2. Of those that a mesh axis runs over, the one named last changes fastest.
Arguments:
- node_feats: bfloat16 [256, 131072], P('feat', 'rows'), may hold values from -6 to 6
- tile_vals: bfloat16 [1024, 16, 128, 128], P('rows'), may hold values from -0.125 to 0.125
- tile_cols: int32 [1024, 16], P('rows'), may hold values from 0 to 1023, as said below
- weight: bfloat16 [256, 256], P(None, 'feat'), may hold values from -0.375 to 0.375
- bias_vec: float32 [256], P('feat'), may hold values from -3 to 3
- grad_out: bfloat16 [256, 131072], P('feat', 'rows'), may hold values from -6 to 6
Outputs:
- activated: bfloat16 [256, 131072], P('feat', 'rows')
- grad_feats: float32 [256, 131072], P('feat', 'rows')
- grad_weight: float32 [256, 256], P(None, 'feat')
- grad_bias: float32 [256], P('feat')
The draws below stay inside these ranges and needn't reach their ends.
Inputs may be any that keep to these rules, and one draw needn't show every extreme that they name: `tile_cols`: among the tiles of one device's 32 blocks of rows, the column blocks held by any one owner (blocks o * 32 to o * 32 + 31) are at most 16 distinct ones and at least one; on every device some owner reaches 16.
All inputs are finite; a program needn't handle non-finite values.
Results may differ from the reference program's by a relative error of at most 0.007.
Values may be sent and summed in bfloat16 or wider, within the bound.
No kernel may reach another device: no remote copies, remote signals or barrier semaphores. Data moves between devices by JAX's collectives and lax.ppermute only.
A program may use at most 256 MiB of HBM per device.

```python
import jax
import jax.numpy as jnp
from jax import lax

FEAT = 256
TB = 128
SLOTS = 16
BLK_DEV = 32
CAP = 16
NODE_BLOCKS = 1024
NODES = 131072
N_ROWS = 32


def draw_tile_cols(key, part):
    keys = jax.random.split(key, 6)
    row_devs = NODE_BLOCKS // BLK_DEV
    tiles = BLK_DEV * SLOTS
    listed = row_devs * CAP
    counts = jax.random.randint(keys[0], (row_devs, row_devs), 1, CAP + 1)
    full_owner = jax.random.randint(keys[1], (row_devs,), 0, row_devs)
    counts = jnp.where(jnp.arange(row_devs)[None, :] == full_owner[:, None], CAP, counts)
    scores = jax.random.randint(keys[2], (row_devs, row_devs, BLK_DEV), 0, 1 << 20) * BLK_DEV + jnp.arange(BLK_DEV)
    orders = jnp.argsort(scores, axis=-1)
    entries = jnp.arange(listed)
    entry_owner = entries // CAP
    entry_rank = entries % CAP
    valid = entry_rank[None, :] < counts[:, entry_owner]
    spare_owner = jax.random.randint(keys[3], (row_devs, tiles), 0, row_devs)
    spare_draw = jax.random.randint(keys[4], (row_devs, tiles), 0, 1 << 20)
    spare_rank = spare_draw % jnp.take_along_axis(counts, spare_owner, axis=1)
    places = jnp.arange(tiles)
    clipped = jnp.minimum(places, listed - 1)
    use_list = (places < listed)[None, :] & jnp.take(valid, clipped, axis=1)
    owners = jnp.where(use_list, entry_owner[clipped][None, :], spare_owner)
    ranks = jnp.where(use_list, entry_rank[clipped][None, :], spare_rank)
    chosen = orders[jnp.arange(row_devs)[:, None], owners, ranks]
    columns = owners * BLK_DEV + chosen
    shuffle = jax.random.randint(keys[5], (row_devs, tiles), 0, 1 << 20) * tiles + places
    columns = jnp.take_along_axis(columns, jnp.argsort(shuffle, axis=-1), axis=1)
    return columns.reshape(NODE_BLOCKS, SLOTS).astype(jnp.int32)


def level_of(rng, shape, cuts, least, largest):
    gain, own = 1.0, jax.random.fold_in(rng, 6)
    for axis_at, parts in cuts:
        heights = jnp.exp(jax.random.uniform(jax.random.fold_in(own, axis_at), (parts,), jnp.float32, least / len(cuts), largest / len(cuts)))
        gain = gain * jnp.repeat(heights, shape[axis_at] // parts).reshape([-1 if axis == axis_at else 1 for axis in range(len(shape))])
    return gain


def scatter_about(own_key, extent, scale, reach, cuts=(), dtype=jnp.bfloat16):
    loudness = level_of(own_key, extent, cuts, -0.22, 0.18) if cuts else 1.0
    values = jax.random.normal(own_key, extent, jnp.float32) * scale * loudness
    return jnp.minimum(jnp.maximum(values, -reach), reach).astype(dtype)


def setup_inputs(seed: int = 0) -> dict:
    key_list = jax.random.split(jax.random.key(seed), 7)
    return {
        "node_feats": scatter_about(key_list[0], (FEAT, NODES), 1.0, 6.0, ((0, 4), (1, 32))),
        "tile_vals": scatter_about(key_list[1], (NODE_BLOCKS, SLOTS, TB, TB), (SLOTS * TB) ** -0.5, 0.125, ((0, 32),)),
        "tile_cols": draw_tile_cols(jax.random.fold_in(key_list[6], 71), 0),
        "weight": scatter_about(key_list[3], (FEAT, FEAT), FEAT ** -0.5, 0.375, ((1, 4),)),
        "bias_vec": scatter_about(key_list[4], (FEAT,), 0.5, 3.0, ((0, 4),), jnp.float32),
        "grad_out": scatter_about(key_list[5], (FEAT, NODES), 1.0, 6.0, ((0, 4), (1, 32))),
    }


def aggregate(node_feats, tile_vals, tile_cols):
    blocks = node_feats.reshape(FEAT, NODE_BLOCKS, TB)

    def one_device(inputs):
        values, columns = inputs
        chosen = jnp.take(blocks, columns.reshape(-1).astype(jnp.int32), axis=1)
        chosen = chosen.reshape(FEAT, BLK_DEV, SLOTS, TB)
        return jnp.einsum('fisb,isab->fia', chosen.astype(jnp.float32), values.astype(jnp.float32))

    result = lax.map(one_device, (tile_vals.reshape(N_ROWS, BLK_DEV, SLOTS, TB, TB), tile_cols.reshape(N_ROWS, BLK_DEV, SLOTS)))
    return result.transpose(1, 0, 2, 3).reshape(FEAT, NODES)


def spread(back_mix, tile_vals, tile_cols):
    pieces = back_mix.reshape(FEAT, N_ROWS, BLK_DEV, TB).transpose(1, 0, 2, 3)

    def advance(running, inputs):
        mixed, values, columns = inputs
        contrib = jnp.einsum('fia,isab->fisb', mixed.astype(jnp.float32), values.astype(jnp.float32))
        running = running.at[:, columns.reshape(-1).astype(jnp.int32)].add(contrib.reshape(FEAT, BLK_DEV * SLOTS, TB))
        return running, None

    running, _ = lax.scan(advance, jnp.zeros((FEAT, NODE_BLOCKS, TB), jnp.float32), (pieces, tile_vals.reshape(N_ROWS, BLK_DEV, SLOTS, TB, TB), tile_cols.reshape(N_ROWS, BLK_DEV, SLOTS)))
    return running.reshape(FEAT, NODES)


def reference(node_feats, tile_vals, tile_cols, weight, bias_vec, grad_out):
    aggregated = aggregate(node_feats, tile_vals, tile_cols).astype(jnp.bfloat16)
    preact = jnp.dot(weight.T, aggregated, preferred_element_type=jnp.float32) + bias_vec[:, None]
    sigma = jax.nn.sigmoid(preact)
    activated = (preact * sigma).astype(jnp.bfloat16)
    grad_pre = (grad_out.astype(jnp.float32) * sigma * (1.0 + preact * (1.0 - sigma))).astype(jnp.bfloat16)
    grad_weight = jnp.dot(aggregated, grad_pre.T, preferred_element_type=jnp.float32)
    grad_bias = jnp.sum(grad_pre.astype(jnp.float32), axis=1)
    back_mix = jnp.dot(weight, grad_pre, preferred_element_type=jnp.float32).astype(jnp.bfloat16)
    grad_feats = spread(back_mix, tile_vals, tile_cols)
    return activated, grad_feats, grad_weight, grad_bias
```

```python
import functools

import jax
import jax.numpy as jnp
from jax import lax
from jax.experimental import pallas as pl
from jax.experimental.pallas import tpu as pltpu
from jax.sharding import PartitionSpec as P

CAP = 16
TB = 128
MIB = 1 << 20
SIDE = 4
PLANES = 2
NEAR = SIDE * PLANES
PART = NEAR * CAP


def row_perm(dx, dy, dz):
    def index(x, y, z):
        return ((x % SIDE) * SIDE + y % SIDE) * PLANES + z % PLANES

    return [
        (index(x, y, z), index(x + dx, y + dy, z + dz))
        for x in range(SIDE)
        for y in range(SIDE)
        for z in range(PLANES)
    ]


def shift(v, near_axis, near, far):
    return lax.ppermute(v, "rows", row_perm(near, far, 0) if near_axis == 0 else row_perm(far, near, 0))


def pack_kernel(asked_ref, *refs):
    sources, outs = refs[: 2 * SIDE], refs[2 * SIDE :]
    half = sources[0].shape[0] // PLANES
    for h in range(2):
        own, plus, minus = outs[3 * h : 3 * h + 3]
        for far in range(SIDE):
            for p in range(NEAR):
                source = sources[h * SIDE + p // PLANES]
                rows = pl.ds((p % PLANES) * half, half)
                for k in range(CAP):
                    at = pl.multiple_of(asked_ref[h, far, p, k] * TB, TB)
                    place = p * CAP + k
                    if far == 2:
                        out, place = (plus, PART + place) if place < PART // 2 else (minus, PART // 2 + place)
                    else:
                        out = (own, plus, None, minus)[far]
                    out[place] = source[rows, pl.ds(at, TB)]


def pack(asked, sources):
    half = sources[0].shape[0] // PLANES
    vmem = pl.BlockSpec(memory_space=pltpu.VMEM)
    out = pl.pallas_call(
        pack_kernel,
        out_shape=[
            jax.ShapeDtypeStruct((n, half, TB), sources[0].dtype) for n in (PART, PART * 3 // 2, PART * 3 // 2) * 2
        ],
        in_specs=[pl.BlockSpec(memory_space=pltpu.SMEM)] + [vmem] * (2 * SIDE),
        out_specs=[vmem] * 6,
        compiler_params=pltpu.CompilerParams(vmem_limit_bytes=40 * MIB),
        name="pack",
    )(asked, *sources)
    return out[:3], out[3:]


def exchange(messages, sign):
    first = [
        [shift(plus, h, 0, sign), shift(minus, h, 0, -sign)] for h, (_, plus, minus) in enumerate(messages)
    ]
    second = [
        [shift(plus[PART:], h, 0, sign), shift(minus[PART:], h, 0, -sign)] for h, (plus, minus) in enumerate(first)
    ]
    return [[messages[h][0], *first[h], *second[h]] for h in range(2)]


LAID = ((0, PART), (PART, PART), (3 * PART, PART), (2 * PART, PART // 2), (2 * PART + PART // 2, PART // 2))


def aggregate_kernel(slot_a_ref, slot_b_ref, *refs):
    n = len(LAID)
    got, (vals_ref, out_ref, a_ref, b_ref, sem) = refs[: 2 * n], refs[2 * n :]
    step = pl.program_id(0)
    per, slots = vals_ref.shape[:2]

    @pl.when(step == 0)
    def _():
        copies = []
        for j, held in enumerate((a_ref, b_ref)):
            for k, (at, size) in enumerate(LAID):
                copies.append(
                    pltpu.make_async_copy(
                        got[j * n + k].at[pl.ds(0, size)], held.at[pl.ds(at, size)], sem.at[j * n + k]
                    )
                )
        for copy in copies:
            copy.start()
        for copy in copies:
            copy.wait()

    for j in range(per):
        i = step * per + j
        a = jnp.concatenate([a_ref[slot_a_ref[i, s]] for s in range(slots)], axis=1)
        b = jnp.concatenate([b_ref[slot_b_ref[i, s]] for s in range(slots)], axis=1)
        tiles = jnp.concatenate([vals_ref[j, s] for s in range(slots)], axis=1)
        out = lax.dot_general(
            jnp.concatenate([a, b], axis=0), tiles, (((1,), (1,)), ((), ())), preferred_element_type=jnp.float32
        )
        out_ref[:, j * TB : (j + 1) * TB] = out.astype(out_ref.dtype)


def aggregate(slot_a, slot_b, got_a, got_b, vals):
    blocks, slots = slot_a.shape
    half = got_a[0].shape[1]
    per = 4
    return pl.pallas_call(
        aggregate_kernel,
        out_shape=jax.ShapeDtypeStruct((2 * half, blocks * TB), jnp.bfloat16),
        grid_spec=pltpu.PrefetchScalarGridSpec(
            num_scalar_prefetch=2,
            grid=(blocks // per,),
            in_specs=[pl.BlockSpec(memory_space=pl.ANY)] * (2 * len(LAID))
            + [pl.BlockSpec((per, slots, TB, TB), lambda i, a, b: (i, 0, 0, 0))],
            out_specs=pl.BlockSpec((2 * half, per * TB), lambda i, a, b: (0, i)),
            scratch_shapes=[pltpu.VMEM((SIDE * PART, half, TB), jnp.bfloat16)] * 2
            + [pltpu.SemaphoreType.DMA((2 * len(LAID),))],
        ),
        compiler_params=pltpu.CompilerParams(vmem_limit_bytes=40 * MIB),
        name="aggregate",
    )(slot_a, slot_b, *got_a, *got_b, vals)


def spread_kernel(slot_a_ref, slot_b_ref, mix_ref, vals_ref, *refs):
    outs, (a_ref, b_ref) = refs[:6], refs[6:]
    step = pl.program_id(0)
    per, slots = vals_ref.shape[:2]
    half = a_ref.shape[1]

    @pl.when(step == 0)
    def _():
        a_ref[...] = jnp.zeros_like(a_ref)
        b_ref[...] = jnp.zeros_like(b_ref)

    for j in range(per):
        i = step * per + j
        mix = mix_ref[:, j * TB : (j + 1) * TB]
        for s in range(slots):
            term = jnp.dot(mix, vals_ref[j, s], preferred_element_type=jnp.float32)
            a_ref[slot_a_ref[i, s]] += term[:half]
            b_ref[slot_b_ref[i, s]] += term[half:]

    @pl.when(step == pl.num_programs(0) - 1)
    def _():
        for j, held in enumerate((a_ref, b_ref)):
            own, plus, minus = outs[3 * j : 3 * j + 3]
            for out, to, (at, size) in zip((own, plus, minus, plus, minus), (0, 0, 0, PART, PART), LAID):
                out[pl.ds(to, size)] = held[pl.ds(at, size)].astype(jnp.bfloat16)


def spread(slot_a, slot_b, mix, vals):
    blocks, slots = slot_a.shape
    half = mix.shape[0] // 2
    per = 4
    out = pl.pallas_call(
        spread_kernel,
        out_shape=[jax.ShapeDtypeStruct((n, half, TB), jnp.bfloat16) for n in (PART, PART * 3 // 2, PART * 3 // 2) * 2],
        grid_spec=pltpu.PrefetchScalarGridSpec(
            num_scalar_prefetch=2,
            grid=(blocks // per,),
            in_specs=[
                pl.BlockSpec((2 * half, per * TB), lambda i, a, b: (0, i)),
                pl.BlockSpec((per, slots, TB, TB), lambda i, a, b: (i, 0, 0, 0)),
            ],
            out_specs=[
                pl.BlockSpec((n, half, TB), lambda i, a, b: (0, 0, 0), pipeline_mode=pl.Buffered(1))
                for n in (PART, PART * 3 // 2, PART * 3 // 2) * 2
            ],
            scratch_shapes=[pltpu.VMEM((SIDE * PART, half, TB), jnp.float32)] * 2,
        ),
        compiler_params=pltpu.CompilerParams(vmem_limit_bytes=48 * MIB),
        name="spread",
    )(slot_a, slot_b, mix, vals)
    return out[:3], out[3:]


def fold_kernel(asked_ref, *refs):
    n = len(LAID)
    got, outs, (acc_ref,) = refs[: 2 * n], refs[2 * n : -1], refs[-1:]
    half = acc_ref.shape[1]
    for h in range(2):
        acc_ref[...] = jnp.zeros_like(acc_ref)
        for held, (at, size) in zip(got[h * n : h * n + n], LAID):
            for j in range(size):
                far, p, k = (at + j) // PART, (at + j) % PART // CAP, (at + j) % CAP
                to = pl.multiple_of(asked_ref[h, far, p, k] * TB, TB)
                acc_ref[p, :, pl.ds(to, TB)] += held[j].astype(jnp.float32)
        for plane in range(PLANES):
            own, plus, minus = outs[(h * PLANES + plane) * 3 :][:3]
            own[...] = acc_ref[plane]
            plus[pl.ds(0, half)] = acc_ref[PLANES + plane].astype(plus.dtype)
            minus[pl.ds(0, half)] = acc_ref[3 * PLANES + plane].astype(minus.dtype)
            plus[pl.ds(half, half // 2)] = acc_ref[2 * PLANES + plane, : half // 2].astype(plus.dtype)
            minus[pl.ds(half, half // 2)] = acc_ref[2 * PLANES + plane, half // 2 :].astype(minus.dtype)


def fold(asked, got, width):
    half = got[0].shape[1]
    vmem = pl.BlockSpec(memory_space=pltpu.VMEM)
    shapes = [
        jax.ShapeDtypeStruct((half, width), jnp.float32),
        jax.ShapeDtypeStruct((half * 3 // 2, width), jnp.bfloat16),
        jax.ShapeDtypeStruct((half * 3 // 2, width), jnp.bfloat16),
    ]
    out = pl.pallas_call(
        fold_kernel,
        out_shape=shapes * (2 * PLANES),
        in_specs=[pl.BlockSpec(memory_space=pltpu.SMEM)] + [vmem] * len(got),
        out_specs=[vmem] * (6 * PLANES),
        scratch_shapes=[pltpu.VMEM((NEAR, half, width), jnp.float32)],
        compiler_params=pltpu.CompilerParams(vmem_limit_bytes=48 * MIB),
        name="fold",
    )(asked, *got)
    return [[out[(h * PLANES + plane) * 3 :][:3] for plane in range(PLANES)] for h in range(2)]


def line_sum(parts, h):
    own, plus, minus = parts
    half = own.shape[0]
    plus, minus = shift(plus, h, 1, 0), shift(minus, h, -1, 0)
    upper, lower = shift(plus[half:], h, 1, 0), shift(minus[half:], h, -1, 0)
    passed = jnp.concatenate([upper, lower], axis=0).astype(jnp.float32)
    return own + plus[:half].astype(jnp.float32) + minus[:half].astype(jnp.float32) + passed


def requests(cols, owners, blocks):
    flat = cols.reshape(-1)
    hit = flat[:, None] == jnp.arange(owners * blocks, dtype=jnp.int32)[None, :]
    named = jnp.any(hit, axis=0).reshape(owners, blocks)
    before = jnp.arange(blocks)[:, None] < jnp.arange(blocks)[None, :]
    rank = jnp.sum(jnp.where(named[:, :, None] & before[None], 1, 0), axis=1).astype(jnp.int32)
    at = named[:, None, :] & (rank[:, None, :] == jnp.arange(CAP, dtype=jnp.int32)[None, :, None])
    wanted = jnp.sum(jnp.where(at, jnp.arange(blocks, dtype=jnp.int32)[None, None, :], 0), axis=2)
    place = jnp.sum(jnp.where(hit, rank.reshape(1, -1), 0), axis=1).astype(jnp.int32)
    return wanted.astype(jnp.int32), place.reshape(cols.shape)


def relative(table, x, y, z):
    for axis, (mine, size) in enumerate(((x, SIDE), (y, SIDE), (z, PLANES))):
        doubled = jnp.concatenate([table, table], axis=axis)
        table = lax.dynamic_slice_in_dim(doubled, mine, size, axis=axis)
    return table


def from_feat(v, step):
    return lax.ppermute(v, "feat", [(i, i ^ step) for i in range(4)])


def every_feat(v):
    two = from_feat(v, 2)
    return v, from_feat(v, 1), two, from_feat(two, 1)


def total_over_rows(v):
    pairs = []
    for dx, dy, dz in ((0, 0, 1), (0, 1, 0), (0, 2, 0), (1, 0, 0), (2, 0, 0)):
        pairs.append(
            [
                ((x * SIDE + y) * PLANES + z, ((x ^ dx) * SIDE + (y ^ dy)) * PLANES + (z ^ dz))
                for x in range(SIDE)
                for y in range(SIDE)
                for z in range(PLANES)
            ]
        )
    for perm in pairs:
        v = v + lax.ppermute(v, "rows", perm)
    return v


def blocks_by_feat(v, mine):
    size = v.shape[0] // 4
    return jnp.concatenate([lax.dynamic_slice_in_dim(v, (mine ^ j) * size, size, axis=0) for j in range(4)], axis=0)


def on_device(node_feats, tile_vals, tile_cols, weight, bias_vec, grad_out):
    feat_loc, width = node_feats.shape
    own_blocks = tile_cols.shape[0]
    half = feat_loc // 2
    me = lax.axis_index("rows")
    x, y, z = me // NEAR, (me // PLANES) % SIDE, me % PLANES
    mine = lax.axis_index("feat")

    other = lax.ppermute(node_feats, "rows", row_perm(0, 0, 1))
    wanted, place = requests(tile_cols, SIDE * NEAR, own_blocks)
    owner = tile_cols // own_blocks
    dx, dy = (owner // NEAR - x) % SIDE, ((owner // PLANES) % SIDE - y) % SIDE
    dz = (owner - z) % PLANES
    slots = [
        ((far * SIDE + near) * PLANES + dz) * CAP + place for near, far in ((dx, dy), (dy, dx))
    ]
    by_place = relative(wanted.reshape(SIDE, SIDE, PLANES, CAP), x, y, z)
    tables = [by_place.transpose(1, 0, 2, 3).reshape(SIDE, NEAR, CAP), by_place.reshape(SIDE, NEAR, CAP)]
    asked = jnp.stack(
        [
            jnp.stack([tables[h][0]] + [shift(tables[h][far], h, 0, far) for far in range(1, SIDE)])
            for h in range(2)
        ]
    )
    other, grad_out = lax.optimization_barrier((other, grad_out))

    lines = []
    for h in range(2):
        own = jnp.concatenate([node_feats[h * half : (h + 1) * half], other[h * half : (h + 1) * half]], axis=0)
        lines += [own] + [shift(own, h, -near, 0) for near in range(1, SIDE)]

    wide = jnp.concatenate([weight.astype(jnp.float32), jnp.broadcast_to(bias_vec[None], (8, feat_loc))], axis=0)
    wide = jnp.concatenate(every_feat(wide), axis=1)
    weight_all = blocks_by_feat(wide[: weight.shape[0]].astype(jnp.bfloat16), mine)
    bias_all = wide[weight.shape[0]]
    grad_out_all = jnp.concatenate(every_feat(grad_out), axis=0)

    got = exchange(pack(asked, lines), -1)
    aggregated = aggregate(*slots, *got, tile_vals)
    agg_all = jnp.concatenate(every_feat(aggregated), axis=0)
    preact = (
        lax.dot_general(weight_all, agg_all, (((0,), (0,)), ((), ())), preferred_element_type=jnp.float32)
        + bias_all[:, None]
    )
    sigma = jax.nn.sigmoid(preact)
    activated = (preact[:feat_loc] * sigma[:feat_loc]).astype(jnp.bfloat16)
    grad_pre = (grad_out_all.astype(jnp.float32) * sigma * (1.0 + preact * (1.0 - sigma))).astype(jnp.bfloat16)
    back_mix = jnp.dot(weight_all[:feat_loc], grad_pre, preferred_element_type=jnp.float32).astype(jnp.bfloat16)

    terms = spread(*slots, back_mix, tile_vals)

    own_grad = grad_pre[:feat_loc]
    weight_part = lax.dot_general(own_grad, agg_all, (((1,), (1,)), ((), ())), preferred_element_type=jnp.float32)
    bias_part = jnp.sum(own_grad.astype(jnp.float32), axis=1)
    parts = jnp.concatenate([weight_part, jnp.broadcast_to(bias_part[:, None], (feat_loc, TB))], axis=1)
    parts = total_over_rows(parts)
    grad_bias = parts[:, weight.shape[0]]
    grad_weight = blocks_by_feat(parts[:, : weight.shape[0]].T, mine)

    back = exchange(terms, 1)
    folded = fold(asked, back[0] + back[1], width)
    ends = [
        jnp.concatenate([line_sum(folded[h][plane], h) for h in range(2)], axis=0) for plane in range(PLANES - 1, -1, -1)
    ]
    arrived = lax.ppermute(ends[0].astype(jnp.bfloat16), "rows", row_perm(0, 0, 1))
    grad_feats = ends[1] + arrived.astype(jnp.float32)
    return (activated, grad_feats, grad_weight, grad_bias)


def solution(mesh):
    placed = (
        P("feat", "rows"),
        P("rows", None, None, None),
        P("rows", None),
        P(None, "feat"),
        P("feat"),
        P("feat", "rows"),
    )
    return jax.shard_map(
        on_device,
        mesh=mesh,
        in_specs=placed,
        out_specs=(P("feat", "rows"), P("feat", "rows"), P(None, "feat"), P("feat")),
        check_vma=False,
    )
```

```python
import functools

import jax
import jax.numpy as jnp
from jax import lax
from jax.experimental import pallas as pl
from jax.experimental.pallas import tpu as pltpu
from jax.sharding import PartitionSpec as P

CAP = 16
BATCH = 8
TB = 128
MIB = 1 << 20
SIDE = 4
PLANES = 2
NEAR = SIDE * PLANES
PART = NEAR * CAP


def row_perm(dx, dy, dz):
    def index(x, y, z):
        return ((x % SIDE) * SIDE + y % SIDE) * PLANES + z % PLANES

    return [
        (index(x, y, z), index(x + dx, y + dy, z + dz))
        for x in range(SIDE)
        for y in range(SIDE)
        for z in range(PLANES)
    ]


def shift(v, near_axis, near, far):
    return lax.ppermute(v, "rows", row_perm(near, far, 0) if near_axis == 0 else row_perm(far, near, 0))


def pack_kernel(asked_ref, *refs):
    outs = refs[-6:]
    half = refs[0].shape[0] // PLANES
    for h in range(2):
        own, plus, minus = outs[3 * h : 3 * h + 3]
        near, plus_near, minus_near, upper, lower = refs[5 * h : 5 * h + 5]
        parts = [pl.ds(plane * half, half) for plane in range(PLANES)]
        sources = [held.at[rows] for held in (near, plus_near) for rows in parts]
        sources += [upper, lower] + [minus_near.at[rows] for rows in parts]
        for far in range(SIDE):
            for p in range(NEAR):
                source = sources[p]
                for k in range(CAP):
                    at = pl.multiple_of(asked_ref[h, far, p, k] * TB, TB)
                    place = p * CAP + k
                    if far == 2:
                        out, place = (plus, PART + place) if place < PART // 2 else (minus, PART // 2 + place)
                    else:
                        out = (own, plus, None, minus)[far]
                    out[place] = source[:, pl.ds(at, TB)]


def pack(asked, sources):
    half = sources[0].shape[0] // 2
    vmem = pl.BlockSpec(memory_space=pltpu.VMEM)
    out = pl.pallas_call(
        pack_kernel,
        out_shape=[
            jax.ShapeDtypeStruct((n, half, TB), sources[0].dtype) for n in (PART, PART * 3 // 2, PART * 3 // 2) * 2
        ],
        in_specs=[pl.BlockSpec(memory_space=pltpu.SMEM)] + [vmem] * len(sources),
        out_specs=[vmem] * 6,
        compiler_params=pltpu.CompilerParams(vmem_limit_bytes=40 * MIB),
        name="pack",
    )(asked, *sources)
    return out[:3], out[3:]


def exchange(messages, sign, side=None):
    first = [
        [shift(plus, h, 0, sign), shift(minus, h, 0, -sign)] for h, (_, plus, minus) in enumerate(messages)
    ]
    if side is not None:
        first, side = lax.optimization_barrier((first, side))
    second = [
        [shift(plus[PART:], h, 0, sign), shift(minus[PART:], h, 0, -sign)] for h, (plus, minus) in enumerate(first)
    ]
    return [[messages[h][0], *first[h], *second[h]] for h in range(2)], side


LAID = ((0, PART), (PART, PART), (3 * PART, PART), (2 * PART, PART // 2), (2 * PART + PART // 2, PART // 2))


def aggregate_kernel(slot_a_ref, slot_b_ref, *refs):
    n = len(LAID)
    got, (vals_ref, out_ref, a_ref, b_ref, sem) = refs[: 2 * n], refs[2 * n :]
    step = pl.program_id(0)
    per, slots = vals_ref.shape[:2]

    @pl.when(step == 0)
    def _():
        copies = []
        for j, held in enumerate((a_ref, b_ref)):
            for k, (at, size) in enumerate(LAID):
                copies.append(
                    pltpu.make_async_copy(
                        got[j * n + k].at[pl.ds(0, size)], held.at[pl.ds(at, size)], sem.at[j * n + k]
                    )
                )
        for copy in copies:
            copy.start()
        for copy in copies:
            copy.wait()

    for j in range(per):
        i = step * per + j
        a = jnp.concatenate([a_ref[slot_a_ref[i, s]] for s in range(slots)], axis=1)
        b = jnp.concatenate([b_ref[slot_b_ref[i, s]] for s in range(slots)], axis=1)
        tiles = jnp.concatenate([vals_ref[j, s] for s in range(slots)], axis=1)
        out = lax.dot_general(
            jnp.concatenate([a, b], axis=0), tiles, (((1,), (1,)), ((), ())), preferred_element_type=jnp.float32
        )
        out_ref[:, j * TB : (j + 1) * TB] = out.astype(out_ref.dtype)


def aggregate(slot_a, slot_b, got_a, got_b, vals):
    blocks, slots = slot_a.shape
    half = got_a[0].shape[1]
    per = 4
    return pl.pallas_call(
        aggregate_kernel,
        out_shape=jax.ShapeDtypeStruct((2 * half, blocks * TB), jnp.bfloat16),
        grid_spec=pltpu.PrefetchScalarGridSpec(
            num_scalar_prefetch=2,
            grid=(blocks // per,),
            in_specs=[pl.BlockSpec(memory_space=pltpu.HBM)] * (2 * len(LAID))
            + [pl.BlockSpec((per, slots, TB, TB), lambda i, a, b: (i, 0, 0, 0))],
            out_specs=pl.BlockSpec((2 * half, per * TB), lambda i, a, b: (0, i)),
            scratch_shapes=[pltpu.VMEM((SIDE * PART, half, TB), jnp.bfloat16)] * 2
            + [pltpu.SemaphoreType.DMA((2 * len(LAID),))],
        ),
        compiler_params=pltpu.CompilerParams(vmem_limit_bytes=40 * MIB),
        name="aggregate",
    )(slot_a, slot_b, *got_a, *got_b, vals)


def spread_kernel(slot_a_ref, slot_b_ref, mix_ref, vals_ref, *refs):
    outs, (a_ref, b_ref) = refs[:6], refs[6:]
    step = pl.program_id(0)
    per, slots = vals_ref.shape[:2]
    half = a_ref.shape[1]

    @pl.when(step == 0)
    def _():
        a_ref[...] = jnp.zeros_like(a_ref)
        b_ref[...] = jnp.zeros_like(b_ref)

    for j in range(per):
        i = step * per + j
        mix = mix_ref[:, j * TB : (j + 1) * TB]
        for s in range(slots):
            term = jnp.dot(mix, vals_ref[j, s], preferred_element_type=jnp.float32)
            a_ref[slot_a_ref[i, s]] += term[:half]
            b_ref[slot_b_ref[i, s]] += term[half:]

    @pl.when(step == pl.num_programs(0) - 1)
    def _():
        for j, held in enumerate((a_ref, b_ref)):
            own, plus, minus = outs[3 * j : 3 * j + 3]
            for out, to, (at, size) in zip((own, plus, minus, plus, minus), (0, 0, 0, PART, PART), LAID):
                out[pl.ds(to, size)] = held[pl.ds(at, size)].astype(jnp.bfloat16)


def spread(slot_a, slot_b, mix, vals):
    blocks, slots = slot_a.shape
    half = mix.shape[0] // 2
    per = 4
    out = pl.pallas_call(
        spread_kernel,
        out_shape=[jax.ShapeDtypeStruct((n, half, TB), jnp.bfloat16) for n in (PART, PART * 3 // 2, PART * 3 // 2) * 2],
        grid_spec=pltpu.PrefetchScalarGridSpec(
            num_scalar_prefetch=2,
            grid=(blocks // per,),
            in_specs=[
                pl.BlockSpec((2 * half, per * TB), lambda i, a, b: (0, i)),
                pl.BlockSpec((per, slots, TB, TB), lambda i, a, b: (i, 0, 0, 0)),
            ],
            out_specs=[
                pl.BlockSpec((n, half, TB), lambda i, a, b: (0, 0, 0), pipeline_mode=pl.Buffered(1))
                for n in (PART, PART * 3 // 2, PART * 3 // 2) * 2
            ],
            scratch_shapes=[pltpu.VMEM((SIDE * PART, half, TB), jnp.float32)] * 2,
        ),
        compiler_params=pltpu.CompilerParams(vmem_limit_bytes=48 * MIB),
        name="spread",
    )(slot_a, slot_b, mix, vals)
    return out[:3], out[3:]


def fold_kernel(asked_ref, *refs):
    n = len(LAID)
    got, outs, (acc_ref,) = refs[: 2 * n], refs[2 * n : -1], refs[-1:]
    p = pl.program_id(0)
    for h in range(2):
        acc_ref[...] = jnp.zeros_like(acc_ref)

        def add(held, far):
            for start in range(CAP - BATCH, -1, -BATCH):
                at = [
                    pl.ds(pl.multiple_of(asked_ref[h, far, p, k] * TB, TB), TB) for k in range(start, start + BATCH)
                ]
                sums = [acc_ref[:, to] + held[start + j].astype(jnp.float32) for j, to in enumerate(at)]
                for to, total in reversed(list(zip(at, sums))):
                    acc_ref[:, to] = total

        own, plus, minus, upper, lower = got[h * n : h * n + n]
        for held, far in ((own, 0), (plus, 1), (minus, 3)):
            add(held, far)
        pl.when(p < NEAR // 2)(functools.partial(add, upper, 2))
        pl.when(p >= NEAR // 2)(functools.partial(add, lower, 2))
        for plane in range(PLANES):
            own, plus, minus = outs[(h * PLANES + plane) * 3 :][:3]
            half = own.shape[0]

            @pl.when(p == plane)
            def _():
                own[...] = acc_ref[...]

            @pl.when(p == PLANES + plane)
            def _():
                plus[:half] = acc_ref[...].astype(plus.dtype)

            @pl.when(p == 2 * PLANES + plane)
            def _():
                plus[half:] = acc_ref[: half // 2].astype(plus.dtype)
                minus[half:] = acc_ref[half // 2 :].astype(minus.dtype)

            @pl.when(p == 3 * PLANES + plane)
            def _():
                minus[:half] = acc_ref[...].astype(minus.dtype)


def fold(asked, got, width):
    half = got[0].shape[1]
    block = (CAP, half, TB)
    specs = [pl.BlockSpec(block, lambda p, a: (p, 0, 0))] * 3 + [
        pl.BlockSpec(block, lambda p, a: (jnp.minimum(p, NEAR // 2 - 1), 0, 0)),
        pl.BlockSpec(block, lambda p, a: (jnp.maximum(p - NEAR // 2, 0), 0, 0)),
    ]
    out = pl.pallas_call(
        fold_kernel,
        out_shape=[
            jax.ShapeDtypeStruct((half, width), jnp.float32),
            jax.ShapeDtypeStruct((half * 3 // 2, width), jnp.bfloat16),
            jax.ShapeDtypeStruct((half * 3 // 2, width), jnp.bfloat16),
        ]
        * (2 * PLANES),
        grid_spec=pltpu.PrefetchScalarGridSpec(
            num_scalar_prefetch=1,
            grid=(NEAR,),
            in_specs=specs * 2,
            out_specs=[
                pl.BlockSpec((rows, width), lambda p, a: (0, 0), pipeline_mode=pl.Buffered(1))
                for rows in (half, half * 3 // 2, half * 3 // 2) * (2 * PLANES)
            ],
            scratch_shapes=[pltpu.VMEM((half, width), jnp.float32)],
        ),
        compiler_params=pltpu.CompilerParams(vmem_limit_bytes=40 * MIB),
        name="fold",
    )(asked, *got)
    return [[out[(h * PLANES + plane) * 3 :][:3] for plane in range(PLANES)] for h in range(2)]


def line_sum(folded, plane, side=None):
    first = [
        [shift(parts[plane][1], h, 1, 0), shift(parts[plane][2], h, -1, 0)] for h, parts in enumerate(folded)
    ]
    if side is not None:
        first, side = lax.optimization_barrier((first, side))
    sums = []
    for h, (plus, minus) in enumerate(first):
        own = folded[h][plane][0]
        half = own.shape[0]
        passed = [shift(plus[half:], h, 1, 0), shift(minus[half:], h, -1, 0)]
        total = own + plus[:half].astype(jnp.float32) + minus[:half].astype(jnp.float32)
        sums.append(total + jnp.concatenate(passed, axis=0).astype(jnp.float32))
    return jnp.concatenate(sums, axis=0), side


def requests(cols, owners, blocks):
    flat = cols.reshape(-1)
    hit = flat[:, None] == jnp.arange(owners * blocks, dtype=jnp.int32)[None, :]
    named = jnp.any(hit, axis=0).reshape(owners, blocks)
    before = jnp.arange(blocks)[:, None] < jnp.arange(blocks)[None, :]
    rank = jnp.sum(jnp.where(named[:, :, None] & before[None], 1, 0), axis=1).astype(jnp.int32)
    at = named[:, None, :] & (rank[:, None, :] == jnp.arange(CAP, dtype=jnp.int32)[None, :, None])
    wanted = jnp.sum(jnp.where(at, jnp.arange(blocks, dtype=jnp.int32)[None, None, :], 0), axis=2)
    place = jnp.sum(jnp.where(hit, rank.reshape(1, -1), 0), axis=1).astype(jnp.int32)
    return wanted.astype(jnp.int32), place.reshape(cols.shape)


def relative(table, x, y, z):
    for axis, (mine, size) in enumerate(((x, SIDE), (y, SIDE), (z, PLANES))):
        doubled = jnp.concatenate([table, table], axis=axis)
        table = lax.dynamic_slice_in_dim(doubled, mine, size, axis=axis)
    return table


def from_feat(v, step):
    return lax.ppermute(v, "feat", [(i, i ^ step) for i in range(4)])


def every_feat(v):
    two = from_feat(v, 2)
    return v, from_feat(v, 1), two, from_feat(two, 1)


def row_swap(v, dx, dy, dz):
    pairs = [
        ((x * SIDE + y) * PLANES + z, ((x ^ dx) * SIDE + (y ^ dy)) * PLANES + (z ^ dz))
        for x in range(SIDE)
        for y in range(SIDE)
        for z in range(PLANES)
    ]
    return v + lax.ppermute(v, "rows", pairs)


def blocks_by_feat(v, mine):
    size = v.shape[0] // 4
    return jnp.concatenate([lax.dynamic_slice_in_dim(v, (mine ^ j) * size, size, axis=0) for j in range(4)], axis=0)


def on_device(node_feats, tile_vals, tile_cols, weight, bias_vec, grad_out):
    feat_loc, width = node_feats.shape
    own_blocks = tile_cols.shape[0]
    half = feat_loc // 2
    me = lax.axis_index("rows")
    x, y, z = me // NEAR, (me // PLANES) % SIDE, me % PLANES
    mine = lax.axis_index("feat")

    other = lax.ppermute(node_feats, "rows", row_perm(0, 0, 1))
    wanted, place = requests(tile_cols, SIDE * NEAR, own_blocks)
    owner = tile_cols // own_blocks
    dx, dy = (owner // NEAR - x) % SIDE, ((owner // PLANES) % SIDE - y) % SIDE
    dz = (owner - z) % PLANES
    slots = [
        ((far * SIDE + near) * PLANES + dz) * CAP + place for near, far in ((dx, dy), (dy, dx))
    ]
    by_place = relative(wanted.reshape(SIDE, SIDE, PLANES, CAP), x, y, z)
    tables = [by_place.transpose(1, 0, 2, 3).reshape(SIDE, NEAR, CAP), by_place.reshape(SIDE, NEAR, CAP)]
    shards = []
    for h in range(2):
        rows = slice(h * half, (h + 1) * half)
        aside = jnp.pad(tables[1 - h].reshape(SIDE, PART).astype(jnp.bfloat16), ((0, feat_loc - SIDE), (0, 0)))
        both = jnp.concatenate([node_feats[rows], other[rows]], axis=0)
        shards.append(jnp.concatenate([both, aside], axis=1))
    first = [[shift(shards[h], h, -1, 0), shift(shards[h], h, 1, 0)] for h in range(2)]
    second = [[shift(first[h][0][:half], h, -1, 0), shift(first[h][1][half:], h, 1, 0)] for h in range(2)]
    lines = [v for h in range(2) for v in (shards[h], *first[h], *second[h])]
    asked = []
    for h in range(2):
        (plus, minus), (upper, _) = first[1 - h], second[1 - h]
        heard = [v[far, width:].astype(jnp.int32) for far, v in ((1, minus), (2, upper), (3, plus))]
        asked.append(jnp.stack([tables[h][0]] + [v.reshape(NEAR, CAP) for v in heard]))
    asked = jnp.stack(asked)
    lines, weight, bias_vec, grad_out = lax.optimization_barrier((lines, weight, bias_vec, grad_out))

    wide = jnp.concatenate([weight.astype(jnp.float32), jnp.broadcast_to(bias_vec[None], (8, feat_loc))], axis=0)
    wide = jnp.concatenate(every_feat(wide), axis=1)
    weight_all = blocks_by_feat(wide[: weight.shape[0]].astype(jnp.bfloat16), mine)
    bias_all = wide[weight.shape[0]]
    grad_out_all = jnp.concatenate(every_feat(grad_out), axis=0)

    got, _ = exchange(pack(asked, lines), -1)
    aggregated = aggregate(*slots, *got, tile_vals)
    agg_all = jnp.concatenate(every_feat(aggregated), axis=0)
    preact = (
        lax.dot_general(weight_all, agg_all, (((0,), (0,)), ((), ())), preferred_element_type=jnp.float32)
        + bias_all[:, None]
    )
    sigma = jax.nn.sigmoid(preact)
    activated = (preact[:feat_loc] * sigma[:feat_loc]).astype(jnp.bfloat16)
    grad_pre = (grad_out_all.astype(jnp.float32) * sigma * (1.0 + preact * (1.0 - sigma))).astype(jnp.bfloat16)
    back_mix = jnp.dot(weight_all[:feat_loc], grad_pre, preferred_element_type=jnp.float32).astype(jnp.bfloat16)

    terms = spread(*slots, back_mix, tile_vals)

    own_grad = grad_pre[:feat_loc]
    weight_part = lax.dot_general(own_grad, agg_all, (((1,), (1,)), ((), ())), preferred_element_type=jnp.float32)
    bias_part = jnp.sum(own_grad.astype(jnp.float32), axis=1)
    bias_rows = jnp.broadcast_to(jnp.pad(bias_part, (0, weight.shape[0] - feat_loc))[None], (8, weight.shape[0]))
    parts = jnp.concatenate([weight_part, bias_rows], axis=0)
    for step in ((0, 0, 1), (0, 1, 0)):
        parts = row_swap(parts, *step)

    back, parts = exchange(terms, 1, parts)
    parts = row_swap(parts, 0, 2, 0)
    back, parts = lax.optimization_barrier((back, parts))
    folded = fold(asked, back[0] + back[1], width)
    passed, parts = line_sum(folded, 1, row_swap(parts, 1, 0, 0))
    passed, parts = passed.astype(jnp.bfloat16), row_swap(parts, 2, 0, 0)
    passed, folded, parts = lax.optimization_barrier((passed, folded, parts))
    arrived = lax.ppermute(passed, "rows", row_perm(0, 0, 1))
    grad_feats = line_sum(folded, 0)[0] + arrived.astype(jnp.float32)
    grad_bias = parts[feat_loc, :feat_loc]
    grad_weight = blocks_by_feat(parts[:feat_loc].T, mine)
    return (activated, grad_feats, grad_weight, grad_bias)


def solution(mesh):
    placed = (
        P("feat", "rows"),
        P("rows", None, None, None),
        P("rows", None),
        P(None, "feat"),
        P("feat"),
        P("feat", "rows"),
    )
    return jax.shard_map(
        on_device,
        mesh=mesh,
        in_specs=placed,
        out_specs=(P("feat", "rows"), P("feat", "rows"), P(None, "feat"), P("feat")),
        check_vma=False,
    )
```

```python
import functools

import jax
import jax.numpy as jnp
from jax import lax
from jax.experimental import pallas as pl
from jax.experimental.pallas import tpu as pltpu
from jax.sharding import PartitionSpec as P

CAP = 16
BATCH = 8
TB = 128
MIB = 1 << 20
SIDE = 4
PLANES = 2
NEAR = SIDE * PLANES
PART = NEAR * CAP


def row_perm(dx, dy, dz):
    def index(x, y, z):
        return ((x % SIDE) * SIDE + y % SIDE) * PLANES + z % PLANES

    return [
        (index(x, y, z), index(x + dx, y + dy, z + dz))
        for x in range(SIDE)
        for y in range(SIDE)
        for z in range(PLANES)
    ]


def shift(v, near_axis, near, far):
    return lax.ppermute(v, "rows", row_perm(near, far, 0) if near_axis == 0 else row_perm(far, near, 0))


def in_hbm(*arrays):
    return [pltpu.with_memory_space_constraint(v, pltpu.HBM) for v in arrays]


def pack_kernel(asked_ref, *refs):
    outs = refs[-6:]
    half = refs[0].shape[0] // PLANES
    for h in range(2):
        own, plus, minus = outs[3 * h : 3 * h + 3]
        near, plus_near, minus_near, upper, lower = refs[5 * h : 5 * h + 5]
        parts = [pl.ds(plane * half, half) for plane in range(PLANES)]
        sources = [held.at[rows] for held in (near, plus_near) for rows in parts]
        sources += [upper, lower] + [minus_near.at[rows] for rows in parts]
        for far in range(SIDE):
            for p in range(NEAR):
                source = sources[p]
                for k in range(CAP):
                    at = pl.multiple_of(asked_ref[h, far, p, k] * TB, TB)
                    place = p * CAP + k
                    if far == 2:
                        out, place = (plus, PART + place) if place < PART // 2 else (minus, PART // 2 + place)
                    else:
                        out = (own, plus, None, minus)[far]
                    out[place] = source[:, pl.ds(at, TB)]


def pack(asked, sources):
    half = sources[0].shape[0] // 2
    vmem = pl.BlockSpec(memory_space=pltpu.VMEM)
    out = pl.pallas_call(
        pack_kernel,
        out_shape=[
            jax.ShapeDtypeStruct((n, half, TB), sources[0].dtype) for n in (PART, PART * 3 // 2, PART * 3 // 2) * 2
        ],
        in_specs=[pl.BlockSpec(memory_space=pltpu.SMEM)] + [vmem] * len(sources),
        out_specs=[vmem] * 6,
        compiler_params=pltpu.CompilerParams(vmem_limit_bytes=18 * MIB),
        name="pack",
    )(asked, *sources)
    return out[:3], out[3:]


def exchange(messages, sign, side=None):
    first = [
        [shift(plus, h, 0, sign), shift(minus, h, 0, -sign)] for h, (_, plus, minus) in enumerate(messages)
    ]
    if side is not None:
        first, side = lax.optimization_barrier((first, side))
    second = [
        [shift(plus[PART:], h, 0, sign), shift(minus[PART:], h, 0, -sign)] for h, (plus, minus) in enumerate(first)
    ]
    return [[messages[h][0], *first[h], *second[h]] for h in range(2)], side


LAID = ((0, PART), (PART, PART), (3 * PART, PART), (2 * PART, PART // 2), (2 * PART + PART // 2, PART // 2))


def aggregate_kernel(slot_a_ref, slot_b_ref, *refs):
    n = len(LAID)
    got, (vals_ref, out_ref, a_ref, b_ref, sem) = refs[: 2 * n], refs[2 * n :]
    step = pl.program_id(0)
    per, slots = vals_ref.shape[:2]

    @pl.when(step == 0)
    def _():
        copies = []
        for j, held in enumerate((a_ref, b_ref)):
            for k, (at, size) in enumerate(LAID):
                copies.append(
                    pltpu.make_async_copy(
                        got[j * n + k].at[pl.ds(0, size)], held.at[pl.ds(at, size)], sem.at[j * n + k]
                    )
                )
        for copy in copies:
            copy.start()
        for copy in copies:
            copy.wait()

    for j in range(per):
        i = step * per + j
        a = jnp.concatenate([a_ref[slot_a_ref[i, s]] for s in range(slots)], axis=1)
        b = jnp.concatenate([b_ref[slot_b_ref[i, s]] for s in range(slots)], axis=1)
        tiles = jnp.concatenate([vals_ref[j, s] for s in range(slots)], axis=1)
        out = lax.dot_general(
            tiles, jnp.concatenate([a, b], axis=0), (((1,), (1,)), ((), ())), preferred_element_type=jnp.float32
        )
        out_ref[:, j * TB : (j + 1) * TB] = out.T.astype(out_ref.dtype)


def aggregate(slot_a, slot_b, got_a, got_b, vals):
    blocks, slots = slot_a.shape
    half = got_a[0].shape[1]
    per = 4
    return pl.pallas_call(
        aggregate_kernel,
        out_shape=jax.ShapeDtypeStruct((2 * half, blocks * TB), jnp.bfloat16),
        grid_spec=pltpu.PrefetchScalarGridSpec(
            num_scalar_prefetch=2,
            grid=(blocks // per,),
            in_specs=[pl.BlockSpec(memory_space=pltpu.HBM)] * (2 * len(LAID))
            + [pl.BlockSpec((per, slots, TB, TB), lambda i, a, b: (i, 0, 0, 0))],
            out_specs=pl.BlockSpec((2 * half, per * TB), lambda i, a, b: (0, i)),
            scratch_shapes=[pltpu.VMEM((SIDE * PART, half, TB), jnp.bfloat16)] * 2
            + [pltpu.SemaphoreType.DMA((2 * len(LAID),))],
        ),
        compiler_params=pltpu.CompilerParams(vmem_limit_bytes=16 * MIB),
        name="aggregate",
    )(slot_a, slot_b, *in_hbm(*got_a, *got_b, vals))


def spread_kernel(slot_a_ref, slot_b_ref, mix_ref, vals_ref, *refs):
    outs, (a_ref, b_ref) = refs[:6], refs[6:]
    step = pl.program_id(0)
    per, slots = vals_ref.shape[:2]
    half = a_ref.shape[1]

    @pl.when(step == 0)
    def _():
        a_ref[...] = jnp.zeros_like(a_ref)
        b_ref[...] = jnp.zeros_like(b_ref)

    for j in range(per):
        i = step * per + j
        mix = mix_ref[:, j * TB : (j + 1) * TB]
        tiles = jnp.concatenate([vals_ref[j, s] for s in range(slots)], axis=1)
        terms = jnp.dot(mix, tiles, preferred_element_type=jnp.float32)
        for s in range(slots):
            term = terms[:, s * TB : (s + 1) * TB]
            a_ref[slot_a_ref[i, s]] += term[:half]
            b_ref[slot_b_ref[i, s]] += term[half:]

    @pl.when(step == pl.num_programs(0) - 1)
    def _():
        for j, held in enumerate((a_ref, b_ref)):
            own, plus, minus = outs[3 * j : 3 * j + 3]
            for out, to, (at, size) in zip((own, plus, minus, plus, minus), (0, 0, 0, PART, PART), LAID):
                out[pl.ds(to, size)] = held[pl.ds(at, size)].astype(jnp.bfloat16)


def spread(slot_a, slot_b, mix, vals):
    blocks, slots = slot_a.shape
    half = mix.shape[0] // 2
    per = 4
    out = pl.pallas_call(
        spread_kernel,
        out_shape=[jax.ShapeDtypeStruct((n, half, TB), jnp.bfloat16) for n in (PART, PART * 3 // 2, PART * 3 // 2) * 2],
        grid_spec=pltpu.PrefetchScalarGridSpec(
            num_scalar_prefetch=2,
            grid=(blocks // per,),
            in_specs=[
                pl.BlockSpec((2 * half, per * TB), lambda i, a, b: (0, i)),
                pl.BlockSpec((per, slots, TB, TB), lambda i, a, b: (i, 0, 0, 0)),
            ],
            out_specs=[
                pl.BlockSpec((n, half, TB), lambda i, a, b: (0, 0, 0), pipeline_mode=pl.Buffered(1))
                for n in (PART, PART * 3 // 2, PART * 3 // 2) * 2
            ],
            scratch_shapes=[pltpu.VMEM((SIDE * PART, half, TB), jnp.float32)] * 2,
        ),
        compiler_params=pltpu.CompilerParams(vmem_limit_bytes=34 * MIB),
        name="spread",
    )(slot_a, slot_b, mix, *in_hbm(vals))
    return out[:3], out[3:]


def fold_kernel(asked_ref, *refs):
    n = len(LAID)
    got, outs, (acc_ref,) = refs[: 2 * n], refs[2 * n : -1], refs[-1:]
    p = pl.program_id(0)
    for h in range(2):
        acc_ref[...] = jnp.zeros_like(acc_ref)

        def add(held, far):
            for start in range(CAP - BATCH, -1, -BATCH):
                at = [
                    pl.ds(pl.multiple_of(asked_ref[h, far, p, k] * TB, TB), TB) for k in range(start, start + BATCH)
                ]
                sums = [acc_ref[:, to] + held[start + j].astype(jnp.float32) for j, to in enumerate(at)]
                for to, total in reversed(list(zip(at, sums))):
                    acc_ref[:, to] = total

        own, plus, minus, upper, lower = got[h * n : h * n + n]
        for held, far in ((own, 0), (plus, 1), (minus, 3)):
            add(held, far)
        pl.when(p < NEAR // 2)(functools.partial(add, upper, 2))
        pl.when(p >= NEAR // 2)(functools.partial(add, lower, 2))
        for plane in range(PLANES):
            for near in range(SIDE):

                @pl.when(p == near * PLANES + plane)
                def _():
                    out = outs[(h * PLANES + plane) * SIDE + near]
                    out[...] = acc_ref[...].astype(out.dtype)


def fold(asked, got, width):
    half = got[0].shape[1]
    block = (CAP, half, TB)
    specs = [pl.BlockSpec(block, lambda p, a: (p, 0, 0))] * 3 + [
        pl.BlockSpec(block, lambda p, a: (jnp.minimum(p, NEAR // 2 - 1), 0, 0)),
        pl.BlockSpec(block, lambda p, a: (jnp.maximum(p - NEAR // 2, 0), 0, 0)),
    ]
    out = pl.pallas_call(
        fold_kernel,
        out_shape=([jax.ShapeDtypeStruct((half, width), jnp.float32)]
            + [jax.ShapeDtypeStruct((half, width), jnp.bfloat16)] * (SIDE - 1))
        * (2 * PLANES),
        grid_spec=pltpu.PrefetchScalarGridSpec(
            num_scalar_prefetch=1,
            grid=(NEAR,),
            in_specs=specs * 2,
            out_specs=[pl.BlockSpec((half, width), lambda p, a: (0, 0), pipeline_mode=pl.Buffered(1))] * (2 * NEAR),
            scratch_shapes=[pltpu.VMEM((half, width), jnp.float32)],
        ),
        compiler_params=pltpu.CompilerParams(vmem_limit_bytes=14 * MIB),
        name="fold",
    )(asked, *got)
    return [[out[(h * PLANES + plane) * SIDE :][:SIDE] for plane in range(PLANES)] for h in range(2)]


def line_sum(folded, plane):
    came = {(h, near): shift(folded[h][plane][near], h, near, 0) for near in (2, 1, 3) for h in range(2)}
    sums = []
    for h in range(2):
        total = folded[h][plane][0]
        for near in range(1, SIDE):
            total = total + came[h, near].astype(jnp.float32)
        sums.append(total)
    return jnp.concatenate(sums, axis=0)


def requests(cols, owners, blocks):
    flat = cols.reshape(-1)
    hit = flat[:, None] == jnp.arange(owners * blocks, dtype=jnp.int32)[None, :]
    named = jnp.any(hit, axis=0).reshape(owners, blocks)
    before = jnp.arange(blocks)[:, None] < jnp.arange(blocks)[None, :]
    rank = jnp.sum(jnp.where(named[:, :, None] & before[None], 1, 0), axis=1).astype(jnp.int32)
    at = named[:, None, :] & (rank[:, None, :] == jnp.arange(CAP, dtype=jnp.int32)[None, :, None])
    wanted = jnp.sum(jnp.where(at, jnp.arange(blocks, dtype=jnp.int32)[None, None, :], 0), axis=2)
    place = jnp.sum(jnp.where(hit, rank.reshape(1, -1), 0), axis=1).astype(jnp.int32)
    return wanted.astype(jnp.int32), place.reshape(cols.shape)


def relative(table, x, y, z):
    for axis, (mine, size) in enumerate(((x, SIDE), (y, SIDE), (z, PLANES))):
        doubled = jnp.concatenate([table, table], axis=axis)
        table = lax.dynamic_slice_in_dim(doubled, mine, size, axis=axis)
    return table


def from_feat(v, step):
    return lax.ppermute(v, "feat", [(i, i ^ step) for i in range(4)])


def every_feat(v):
    two = from_feat(v, 2)
    return v, from_feat(v, 1), two, from_feat(two, 1)


def row_swap(v, dx, dy, dz):
    pairs = [
        ((x * SIDE + y) * PLANES + z, ((x ^ dx) * SIDE + (y ^ dy)) * PLANES + (z ^ dz))
        for x in range(SIDE)
        for y in range(SIDE)
        for z in range(PLANES)
    ]
    return v + lax.ppermute(v, "rows", pairs)


def blocks_by_feat(v, mine):
    size = v.shape[0] // 4
    return jnp.concatenate([lax.dynamic_slice_in_dim(v, (mine ^ j) * size, size, axis=0) for j in range(4)], axis=0)


def on_device(node_feats, tile_vals, tile_cols, weight, bias_vec, grad_out):
    feat_loc, width = node_feats.shape
    own_blocks = tile_cols.shape[0]
    half = feat_loc // 2
    me = lax.axis_index("rows")
    x, y, z = me // NEAR, (me // PLANES) % SIDE, me % PLANES
    mine = lax.axis_index("feat")

    other = lax.ppermute(node_feats, "rows", row_perm(0, 0, 1))
    wanted, place = requests(tile_cols, SIDE * NEAR, own_blocks)
    owner = tile_cols // own_blocks
    dx, dy = (owner // NEAR - x) % SIDE, ((owner // PLANES) % SIDE - y) % SIDE
    dz = (owner - z) % PLANES
    slots = [
        ((far * SIDE + near) * PLANES + dz) * CAP + place for near, far in ((dx, dy), (dy, dx))
    ]
    by_place = relative(wanted.reshape(SIDE, SIDE, PLANES, CAP), x, y, z)
    tables = [by_place.transpose(1, 0, 2, 3).reshape(SIDE, NEAR, CAP), by_place.reshape(SIDE, NEAR, CAP)]
    shards = []
    for h in range(2):
        rows = slice(h * half, (h + 1) * half)
        aside = jnp.pad(tables[1 - h].reshape(SIDE, PART).astype(jnp.bfloat16), ((0, feat_loc - SIDE), (0, 0)))
        both = jnp.concatenate([node_feats[rows], other[rows]], axis=0)
        shards.append(jnp.concatenate([both, aside], axis=1))
    first = [[shift(shards[h], h, -1, 0), shift(shards[h], h, 1, 0)] for h in range(2)]
    second = [[shift(first[h][0][:half], h, -1, 0), shift(first[h][1][half:], h, 1, 0)] for h in range(2)]
    lines = [v for h in range(2) for v in (shards[h], *first[h], *second[h])]
    asked = []
    for h in range(2):
        (plus, minus), (upper, _) = first[1 - h], second[1 - h]
        heard = [v[far, width:].astype(jnp.int32) for far, v in ((1, minus), (2, upper), (3, plus))]
        asked.append(jnp.stack([tables[h][0]] + [v.reshape(NEAR, CAP) for v in heard]))
    asked = jnp.stack(asked)
    lines, weight, bias_vec, grad_out = lax.optimization_barrier((lines, weight, bias_vec, grad_out))

    wide = jnp.concatenate([weight.astype(jnp.float32), jnp.broadcast_to(bias_vec[None], (8, feat_loc))], axis=0)
    wide = jnp.concatenate(every_feat(wide), axis=1)
    weight_all = blocks_by_feat(wide[: weight.shape[0]].astype(jnp.bfloat16), mine)
    bias_all = wide[weight.shape[0]]
    grad_out_all = jnp.concatenate(every_feat(grad_out), axis=0)

    got, _ = exchange(pack(asked, lines), -1)
    aggregated = aggregate(*slots, *got, tile_vals)
    agg_all = jnp.concatenate(every_feat(aggregated), axis=0)
    preact = (
        lax.dot_general(weight_all, agg_all, (((0,), (0,)), ((), ())), preferred_element_type=jnp.float32)
        + bias_all[:, None]
    )
    sigma = jax.nn.sigmoid(preact)
    activated = (preact[:feat_loc] * sigma[:feat_loc]).astype(jnp.bfloat16)
    grad_pre = (grad_out_all.astype(jnp.float32) * sigma * (1.0 + preact * (1.0 - sigma))).astype(jnp.bfloat16)
    back_mix = jnp.dot(weight_all[:feat_loc], grad_pre, preferred_element_type=jnp.float32).astype(jnp.bfloat16)

    terms = spread(*slots, back_mix, tile_vals)
    own_grad = grad_pre[:feat_loc]
    weight_part = lax.dot_general(own_grad, agg_all, (((1,), (1,)), ((), ())), preferred_element_type=jnp.float32)
    bias_part = jnp.sum(own_grad.astype(jnp.float32), axis=1)
    bias_rows = jnp.broadcast_to(jnp.pad(bias_part, (0, weight.shape[0] - feat_loc))[None], (8, weight.shape[0]))
    parts = jnp.concatenate([weight_part, bias_rows], axis=0)
    parts = row_swap(row_swap(parts, 0, 0, 1), 0, 1, 0)

    back, parts = exchange(terms, 1, parts)
    parts = row_swap(parts, 0, 2, 0)
    back, parts = lax.optimization_barrier((back, parts))
    folded = fold(asked, back[0] + back[1], width)
    passed, parts = line_sum(folded, 1).astype(jnp.bfloat16), row_swap(parts, 1, 0, 0)
    passed, folded, parts = lax.optimization_barrier((passed, folded, parts))
    arrived = lax.ppermute(passed, "rows", row_perm(0, 0, 1))
    grad_feats = line_sum(folded, 0) + arrived.astype(jnp.float32)
    parts = row_swap(parts, 2, 0, 0)
    grad_bias = parts[feat_loc, :feat_loc]
    grad_weight = blocks_by_feat(parts[:feat_loc].T, mine)
    return (activated, grad_feats, grad_weight, grad_bias)


def solution(mesh):
    placed = (
        P("feat", "rows"),
        P("rows", None, None, None),
        P("rows", None),
        P(None, "feat"),
        P("feat"),
        P("feat", "rows"),
    )
    return jax.shard_map(
        on_device,
        mesh=mesh,
        in_specs=placed,
        out_specs=(P("feat", "rows"), P("feat", "rows"), P(None, "feat"), P("feat")),
        check_vma=False,
    )
```

```python
import functools

import jax
import jax.numpy as jnp
from jax import lax
from jax.experimental import pallas as pl
from jax.experimental.pallas import tpu as pltpu
from jax.sharding import PartitionSpec as P

CAP = 16
BATCH = 8
TB = 128
MIB = 1 << 20
SIDE = 4
PLANES = 2
NEAR = SIDE * PLANES
PART = NEAR * CAP


def row_perm(dx, dy, dz):
    def index(x, y, z):
        return ((x % SIDE) * SIDE + y % SIDE) * PLANES + z % PLANES

    return [
        (index(x, y, z), index(x + dx, y + dy, z + dz))
        for x in range(SIDE)
        for y in range(SIDE)
        for z in range(PLANES)
    ]


def shift(v, near_axis, near, far):
    return lax.ppermute(v, "rows", row_perm(near, far, 0) if near_axis == 0 else row_perm(far, near, 0))


def in_hbm(*arrays):
    return [pltpu.with_memory_space_constraint(v, pltpu.HBM) for v in arrays]


def pack_kernel(asked_ref, *refs):
    outs = refs[-6:]
    half = refs[0].shape[0] // PLANES
    for h in range(2):
        own, plus, minus = outs[3 * h : 3 * h + 3]
        near, plus_near, minus_near, upper, lower = refs[5 * h : 5 * h + 5]
        parts = [pl.ds(plane * half, half) for plane in range(PLANES)]
        sources = [held.at[rows] for held in (near, plus_near) for rows in parts]
        sources += [upper, lower] + [minus_near.at[rows] for rows in parts]
        for far in range(SIDE):
            for p in range(NEAR):
                source = sources[p]
                for k in range(CAP):
                    at = pl.multiple_of(asked_ref[h, far, p, k] * TB, TB)
                    place = p * CAP + k
                    if far == 2:
                        out, place = (plus, PART + place) if place < PART // 2 else (minus, PART // 2 + place)
                    else:
                        out = (own, plus, None, minus)[far]
                    out[place] = source[:, pl.ds(at, TB)]


def pack(asked, sources):
    half = sources[0].shape[0] // 2
    vmem = pl.BlockSpec(memory_space=pltpu.VMEM)
    out = pl.pallas_call(
        pack_kernel,
        out_shape=[
            jax.ShapeDtypeStruct((n, half, TB), sources[0].dtype) for n in (PART, PART * 3 // 2, PART * 3 // 2) * 2
        ],
        in_specs=[pl.BlockSpec(memory_space=pltpu.SMEM)] + [vmem] * len(sources),
        out_specs=[vmem] * 6,
        compiler_params=pltpu.CompilerParams(vmem_limit_bytes=18 * MIB),
        name="pack",
    )(asked, *sources)
    return out[:3], out[3:]


def exchange(messages, sign, side=None):
    first = [
        [shift(plus, h, 0, sign), shift(minus, h, 0, -sign)] for h, (_, plus, minus) in enumerate(messages)
    ]
    if side is not None:
        first, side = lax.optimization_barrier((first, side))
    second = [
        [shift(plus[PART:], h, 0, sign), shift(minus[PART:], h, 0, -sign)] for h, (plus, minus) in enumerate(first)
    ]
    return [[messages[h][0], *first[h], *second[h]] for h in range(2)], side


LAID = ((0, PART), (PART, PART), (3 * PART, PART), (2 * PART, PART // 2), (2 * PART + PART // 2, PART // 2))


def aggregate_kernel(slot_a_ref, slot_b_ref, *refs):
    n = len(LAID)
    got, (vals_ref, out_ref, a_ref, b_ref, sem) = refs[: 2 * n], refs[2 * n :]
    step = pl.program_id(0)
    per, slots = vals_ref.shape[:2]

    @pl.when(step == 0)
    def _():
        copies = []
        for j, held in enumerate((a_ref, b_ref)):
            for k, (at, size) in enumerate(LAID):
                copies.append(
                    pltpu.make_async_copy(
                        got[j * n + k].at[pl.ds(0, size)], held.at[pl.ds(at, size)], sem.at[j * n + k]
                    )
                )
        for copy in copies:
            copy.start()
        for copy in copies:
            copy.wait()

    for j in range(per):
        i = step * per + j
        a = jnp.concatenate([a_ref[slot_a_ref[i, s]] for s in range(slots)], axis=1)
        b = jnp.concatenate([b_ref[slot_b_ref[i, s]] for s in range(slots)], axis=1)
        tiles = jnp.concatenate([vals_ref[j, s] for s in range(slots)], axis=1)
        out = lax.dot_general(
            tiles, jnp.concatenate([a, b], axis=0), (((1,), (1,)), ((), ())), preferred_element_type=jnp.float32
        )
        out_ref[:, j * TB : (j + 1) * TB] = out.T.astype(out_ref.dtype)


def aggregate(slot_a, slot_b, got_a, got_b, vals):
    blocks, slots = slot_a.shape
    half = got_a[0].shape[1]
    per = 4
    return pl.pallas_call(
        aggregate_kernel,
        out_shape=jax.ShapeDtypeStruct((2 * half, blocks * TB), jnp.bfloat16),
        grid_spec=pltpu.PrefetchScalarGridSpec(
            num_scalar_prefetch=2,
            grid=(blocks // per,),
            in_specs=[pl.BlockSpec(memory_space=pltpu.HBM)] * (2 * len(LAID))
            + [pl.BlockSpec((per, slots, TB, TB), lambda i, a, b: (i, 0, 0, 0))],
            out_specs=pl.BlockSpec((2 * half, per * TB), lambda i, a, b: (0, i)),
            scratch_shapes=[pltpu.VMEM((SIDE * PART, half, TB), jnp.bfloat16)] * 2
            + [pltpu.SemaphoreType.DMA((2 * len(LAID),))],
        ),
        compiler_params=pltpu.CompilerParams(vmem_limit_bytes=16 * MIB),
        name="aggregate",
    )(slot_a, slot_b, *in_hbm(*got_a, *got_b, vals))


def spread_kernel(slot_a_ref, slot_b_ref, mix_ref, vals_ref, *refs):
    outs, (a_ref, b_ref) = refs[:6], refs[6:]
    step = pl.program_id(0)
    per, slots = vals_ref.shape[:2]
    half = a_ref.shape[1]

    @pl.when(step == 0)
    def _():
        a_ref[...] = jnp.zeros_like(a_ref)
        b_ref[...] = jnp.zeros_like(b_ref)

    for j in range(per):
        i = step * per + j
        mix = mix_ref[:, j * TB : (j + 1) * TB]
        tiles = jnp.concatenate([vals_ref[j, s] for s in range(slots)], axis=1)
        terms = jnp.dot(mix, tiles, preferred_element_type=jnp.float32)
        for s in range(slots):
            term = terms[:, s * TB : (s + 1) * TB]
            a_ref[slot_a_ref[i, s]] += term[:half]
            b_ref[slot_b_ref[i, s]] += term[half:]

    @pl.when(step == pl.num_programs(0) - 1)
    def _():
        for j, held in enumerate((a_ref, b_ref)):
            own, plus, minus = outs[3 * j : 3 * j + 3]
            for out, to, (at, size) in zip((own, plus, minus, plus, minus), (0, 0, 0, PART, PART), LAID):
                out[pl.ds(to, size)] = held[pl.ds(at, size)].astype(jnp.bfloat16)


def spread(slot_a, slot_b, mix, vals):
    blocks, slots = slot_a.shape
    half = mix.shape[0] // 2
    per = 4
    out = pl.pallas_call(
        spread_kernel,
        out_shape=[jax.ShapeDtypeStruct((n, half, TB), jnp.bfloat16) for n in (PART, PART * 3 // 2, PART * 3 // 2) * 2],
        grid_spec=pltpu.PrefetchScalarGridSpec(
            num_scalar_prefetch=2,
            grid=(blocks // per,),
            in_specs=[
                pl.BlockSpec((2 * half, per * TB), lambda i, a, b: (0, i)),
                pl.BlockSpec((per, slots, TB, TB), lambda i, a, b: (i, 0, 0, 0)),
            ],
            out_specs=[
                pl.BlockSpec((n, half, TB), lambda i, a, b: (0, 0, 0), pipeline_mode=pl.Buffered(1))
                for n in (PART, PART * 3 // 2, PART * 3 // 2) * 2
            ],
            scratch_shapes=[pltpu.VMEM((SIDE * PART, half, TB), jnp.float32)] * 2,
        ),
        compiler_params=pltpu.CompilerParams(vmem_limit_bytes=34 * MIB),
        name="spread",
    )(slot_a, slot_b, mix, *in_hbm(vals))
    return out[:3], out[3:]


def fold_kernel(asked_ref, *refs):
    n = len(LAID)
    got, outs, (acc_ref,) = refs[: 2 * n], refs[2 * n : -1], refs[-1:]
    p = pl.program_id(0)
    for h in range(2):
        acc_ref[...] = jnp.zeros_like(acc_ref)

        def add(held, far):
            for start in range(CAP - BATCH, -1, -BATCH):
                at = [
                    pl.ds(pl.multiple_of(asked_ref[h, far, p, k] * TB, TB), TB) for k in range(start, start + BATCH)
                ]
                sums = [acc_ref[:, to] + held[start + j].astype(jnp.float32) for j, to in enumerate(at)]
                for to, total in reversed(list(zip(at, sums))):
                    acc_ref[:, to] = total

        own, plus, minus, upper, lower = got[h * n : h * n + n]
        for held, far in ((own, 0), (plus, 1), (minus, 3)):
            add(held, far)
        pl.when(p < NEAR // 2)(functools.partial(add, upper, 2))
        pl.when(p >= NEAR // 2)(functools.partial(add, lower, 2))
        for plane in range(PLANES):
            for near in range(SIDE):

                @pl.when(p == near * PLANES + plane)
                def _():
                    out = outs[(h * PLANES + plane) * SIDE + near]
                    out[...] = acc_ref[...].astype(out.dtype)


def fold(asked, got, width):
    half = got[0].shape[1]
    block = (CAP, half, TB)
    specs = [pl.BlockSpec(block, lambda p, a: (p, 0, 0))] * 3 + [
        pl.BlockSpec(block, lambda p, a: (jnp.minimum(p, NEAR // 2 - 1), 0, 0)),
        pl.BlockSpec(block, lambda p, a: (jnp.maximum(p - NEAR // 2, 0), 0, 0)),
    ]
    out = pl.pallas_call(
        fold_kernel,
        out_shape=([jax.ShapeDtypeStruct((half, width), jnp.float32)]
            + [jax.ShapeDtypeStruct((half, width), jnp.bfloat16)] * (SIDE - 1))
        * (2 * PLANES),
        grid_spec=pltpu.PrefetchScalarGridSpec(
            num_scalar_prefetch=1,
            grid=(NEAR,),
            in_specs=specs * 2,
            out_specs=[pl.BlockSpec((half, width), lambda p, a: (0, 0), pipeline_mode=pl.Buffered(1))] * (2 * NEAR),
            scratch_shapes=[pltpu.VMEM((half, width), jnp.float32)],
        ),
        compiler_params=pltpu.CompilerParams(vmem_limit_bytes=14 * MIB),
        name="fold",
    )(asked, *got)
    return [[out[(h * PLANES + plane) * SIDE :][:SIDE] for plane in range(PLANES)] for h in range(2)]


def line_sum(folded, plane):
    came = {(h, near): shift(folded[h][plane][near], h, near, 0) for near in (2, 1, 3) for h in range(2)}
    sums = []
    for h in range(2):
        total = folded[h][plane][0]
        for near in range(1, SIDE):
            total = total + came[h, near].astype(jnp.float32)
        sums.append(total)
    return jnp.concatenate(sums, axis=0)


def requests(cols, owners, blocks):
    flat = cols.reshape(-1)
    hit = flat[:, None] == jnp.arange(owners * blocks, dtype=jnp.int32)[None, :]
    named = jnp.any(hit, axis=0).reshape(owners, blocks)
    before = jnp.arange(blocks)[:, None] < jnp.arange(blocks)[None, :]
    rank = jnp.sum(jnp.where(named[:, :, None] & before[None], 1, 0), axis=1).astype(jnp.int32)
    at = named[:, None, :] & (rank[:, None, :] == jnp.arange(CAP, dtype=jnp.int32)[None, :, None])
    wanted = jnp.sum(jnp.where(at, jnp.arange(blocks, dtype=jnp.int32)[None, None, :], 0), axis=2)
    place = jnp.sum(jnp.where(hit, rank.reshape(1, -1), 0), axis=1).astype(jnp.int32)
    return wanted.astype(jnp.int32), place.reshape(cols.shape)


def relative(table, x, y, z):
    for axis, (mine, size) in enumerate(((x, SIDE), (y, SIDE), (z, PLANES))):
        doubled = jnp.concatenate([table, table], axis=axis)
        table = lax.dynamic_slice_in_dim(doubled, mine, size, axis=axis)
    return table


def from_feat(v, step):
    return lax.ppermute(v, "feat", [(i, i ^ step) for i in range(4)])


def every_feat(v):
    two = from_feat(v, 2)
    return v, from_feat(v, 1), two, from_feat(two, 1)


def row_swap(v, dx, dy, dz):
    pairs = [
        ((x * SIDE + y) * PLANES + z, ((x ^ dx) * SIDE + (y ^ dy)) * PLANES + (z ^ dz))
        for x in range(SIDE)
        for y in range(SIDE)
        for z in range(PLANES)
    ]
    return v + lax.ppermute(v, "rows", pairs)


def blocks_by_feat(v, mine):
    size = v.shape[0] // 4
    return jnp.concatenate([lax.dynamic_slice_in_dim(v, (mine ^ j) * size, size, axis=0) for j in range(4)], axis=0)


def on_device(node_feats, tile_vals, tile_cols, weight, bias_vec, grad_out):
    feat_loc, width = node_feats.shape
    own_blocks = tile_cols.shape[0]
    half = feat_loc // 2
    me = lax.axis_index("rows")
    x, y, z = me // NEAR, (me // PLANES) % SIDE, me % PLANES
    mine = lax.axis_index("feat")

    other = lax.ppermute(node_feats, "rows", row_perm(0, 0, 1))
    wanted, place = requests(tile_cols, SIDE * NEAR, own_blocks)
    owner = tile_cols // own_blocks
    dx, dy = (owner // NEAR - x) % SIDE, ((owner // PLANES) % SIDE - y) % SIDE
    dz = (owner - z) % PLANES
    slots = [
        ((far * SIDE + near) * PLANES + dz) * CAP + place for near, far in ((dx, dy), (dy, dx))
    ]
    by_place = relative(wanted.reshape(SIDE, SIDE, PLANES, CAP), x, y, z)
    tables = [by_place.transpose(1, 0, 2, 3).reshape(SIDE, NEAR, CAP), by_place.reshape(SIDE, NEAR, CAP)]
    shards = []
    for h in range(2):
        rows = slice(h * half, (h + 1) * half)
        aside = jnp.pad(tables[1 - h].reshape(SIDE, PART).astype(jnp.bfloat16), ((0, feat_loc - SIDE), (0, 0)))
        both = jnp.concatenate([node_feats[rows], other[rows]], axis=0)
        shards.append(jnp.concatenate([both, aside], axis=1))
    first = [[shift(shards[h], h, -1, 0), shift(shards[h], h, 1, 0)] for h in range(2)]
    second = [[shift(first[h][0][:half], h, -1, 0), shift(first[h][1][half:], h, 1, 0)] for h in range(2)]
    lines = [v for h in range(2) for v in (shards[h], *first[h], *second[h])]
    asked = []
    for h in range(2):
        (plus, minus), (upper, _) = first[1 - h], second[1 - h]
        heard = [v[far, width:].astype(jnp.int32) for far, v in ((1, minus), (2, upper), (3, plus))]
        asked.append(jnp.stack([tables[h][0]] + [v.reshape(NEAR, CAP) for v in heard]))
    asked = jnp.stack(asked)
    lines, weight, bias_vec, grad_out = lax.optimization_barrier((lines, weight, bias_vec, grad_out))

    wide = jnp.concatenate([weight.astype(jnp.float32), jnp.broadcast_to(bias_vec[None], (8, feat_loc))], axis=0)
    wide = jnp.concatenate(every_feat(wide), axis=1)
    weight_all = blocks_by_feat(wide[: weight.shape[0]].astype(jnp.bfloat16), mine)
    bias_all = wide[weight.shape[0]]
    grad_out_all = jnp.concatenate(every_feat(grad_out), axis=0)

    got, _ = exchange(pack(asked, lines), -1)
    aggregated = aggregate(*slots, *got, tile_vals)
    agg_all = jnp.concatenate(every_feat(aggregated), axis=0)
    preact = (
        lax.dot_general(weight_all, agg_all, (((0,), (0,)), ((), ())), preferred_element_type=jnp.float32)
        + bias_all[:, None]
    )
    sigma = jax.nn.sigmoid(preact)
    activated = (preact[:feat_loc] * sigma[:feat_loc]).astype(jnp.bfloat16)
    grad_pre = (grad_out_all.astype(jnp.float32) * sigma * (1.0 + preact * (1.0 - sigma))).astype(jnp.bfloat16)
    back_mix = jnp.dot(weight_all[:feat_loc], grad_pre, preferred_element_type=jnp.float32).astype(jnp.bfloat16)

    terms = spread(*slots, back_mix, tile_vals)
    own_grad = grad_pre[:feat_loc]
    weight_part = lax.dot_general(own_grad, agg_all, (((1,), (1,)), ((), ())), preferred_element_type=jnp.float32)
    bias_part = jnp.sum(own_grad.astype(jnp.float32), axis=1)
    bias_rows = jnp.broadcast_to(jnp.pad(bias_part, (0, weight.shape[0] - feat_loc))[None], (8, weight.shape[0]))
    parts = jnp.concatenate([weight_part, bias_rows], axis=0)
    parts = row_swap(row_swap(parts, 0, 0, 1), 0, 1, 0)

    back, parts = exchange(terms, 1, parts)
    parts = row_swap(parts, 0, 2, 0)
    back, parts = lax.optimization_barrier((back, parts))
    folded = fold(asked, back[0] + back[1], width)
    passed, parts = line_sum(folded, 1).astype(jnp.bfloat16), parts
    passed, folded, parts = lax.optimization_barrier((passed, folded, parts))
    arrived = lax.ppermute(passed, "rows", row_perm(0, 0, 1))
    grad_feats = line_sum(folded, 0) + arrived.astype(jnp.float32)
    parts = row_swap(row_swap(parts, 1, 0, 0), 2, 0, 0)
    grad_bias = parts[feat_loc, :feat_loc]
    grad_weight = blocks_by_feat(parts[:feat_loc].T, mine)
    return (activated, grad_feats, grad_weight, grad_bias)


def solution(mesh):
    placed = (
        P("feat", "rows"),
        P("rows", None, None, None),
        P("rows", None),
        P(None, "feat"),
        P("feat"),
        P("feat", "rows"),
    )
    return jax.shard_map(
        on_device,
        mesh=mesh,
        in_specs=placed,
        out_specs=(P("feat", "rows"), P("feat", "rows"), P(None, "feat"), P("feat")),
        check_vma=False,
    )
```

```python
import functools

import jax
import jax.numpy as jnp
from jax import lax
from jax.experimental import pallas as pl
from jax.experimental.pallas import tpu as pltpu
from jax.sharding import PartitionSpec as P

CAP = 16
BATCH = 8
TB = 128
MIB = 1 << 20
SIDE = 4
PLANES = 2
NEAR = SIDE * PLANES
PART = NEAR * CAP


def row_perm(dx, dy, dz):
    def index(x, y, z):
        return ((x % SIDE) * SIDE + y % SIDE) * PLANES + z % PLANES

    return [
        (index(x, y, z), index(x + dx, y + dy, z + dz))
        for x in range(SIDE)
        for y in range(SIDE)
        for z in range(PLANES)
    ]


def shift(v, near_axis, near, far):
    return lax.ppermute(v, "rows", row_perm(near, far, 0) if near_axis == 0 else row_perm(far, near, 0))


def in_hbm(*arrays):
    return [pltpu.with_memory_space_constraint(v, pltpu.HBM) for v in arrays]


def pack_kernel(asked_ref, *refs):
    outs = refs[-6:]
    half = refs[0].shape[0] // PLANES
    for h in range(2):
        own, plus, minus = outs[3 * h : 3 * h + 3]
        near, plus_near, minus_near, upper, lower = refs[5 * h : 5 * h + 5]
        parts = [pl.ds(plane * half, half) for plane in range(PLANES)]
        sources = [held.at[rows] for held in (near, plus_near) for rows in parts]
        sources += [upper, lower] + [minus_near.at[rows] for rows in parts]
        for far in range(SIDE):
            for p in range(NEAR):
                source = sources[p]
                for k in range(CAP):
                    at = pl.multiple_of(asked_ref[h, far, p, k] * TB, TB)
                    place = p * CAP + k
                    if far == 2:
                        out, place = (plus, PART + place) if place < PART // 2 else (minus, PART // 2 + place)
                    else:
                        out = (own, plus, None, minus)[far]
                    out[place] = source[:, pl.ds(at, TB)]


def pack(asked, sources):
    half = sources[0].shape[0] // 2
    vmem = pl.BlockSpec(memory_space=pltpu.VMEM)
    out = pl.pallas_call(
        pack_kernel,
        out_shape=[
            jax.ShapeDtypeStruct((n, half, TB), sources[0].dtype) for n in (PART, PART * 3 // 2, PART * 3 // 2) * 2
        ],
        in_specs=[pl.BlockSpec(memory_space=pltpu.SMEM)] + [vmem] * len(sources),
        out_specs=[vmem] * 6,
        compiler_params=pltpu.CompilerParams(vmem_limit_bytes=18 * MIB),
        name="pack",
    )(asked, *sources)
    return out[:3], out[3:]


def exchange(messages, sign, side=None):
    first = [
        [shift(plus, h, 0, sign), shift(minus, h, 0, -sign)] for h, (_, plus, minus) in enumerate(messages)
    ]
    if side is not None:
        first, side = lax.optimization_barrier((first, side))
    second = [
        [shift(plus[PART:], h, 0, sign), shift(minus[PART:], h, 0, -sign)] for h, (plus, minus) in enumerate(first)
    ]
    return [[messages[h][0], *first[h], *second[h]] for h in range(2)], side


LAID = ((0, PART), (PART, PART), (3 * PART, PART), (2 * PART, PART // 2), (2 * PART + PART // 2, PART // 2))


def aggregate_kernel(slot_a_ref, slot_b_ref, *refs):
    n = len(LAID)
    got, (vals_ref, out_ref, a_ref, b_ref, sem) = refs[: 2 * n], refs[2 * n :]
    step = pl.program_id(0)
    per, slots = vals_ref.shape[:2]

    @pl.when(step == 0)
    def _():
        copies = []
        for j, held in enumerate((a_ref, b_ref)):
            for k, (at, size) in enumerate(LAID):
                copies.append(
                    pltpu.make_async_copy(
                        got[j * n + k].at[pl.ds(0, size)], held.at[pl.ds(at, size)], sem.at[j * n + k]
                    )
                )
        for copy in copies:
            copy.start()
        for copy in copies:
            copy.wait()

    for j in range(per):
        i = step * per + j
        a = jnp.concatenate([a_ref[slot_a_ref[i, s]] for s in range(slots)], axis=1)
        b = jnp.concatenate([b_ref[slot_b_ref[i, s]] for s in range(slots)], axis=1)
        tiles = jnp.concatenate([vals_ref[j, s] for s in range(slots)], axis=1)
        out = lax.dot_general(
            tiles, jnp.concatenate([a, b], axis=0), (((1,), (1,)), ((), ())), preferred_element_type=jnp.float32
        )
        out_ref[:, j * TB : (j + 1) * TB] = out.T.astype(out_ref.dtype)


def aggregate(slot_a, slot_b, got_a, got_b, vals):
    blocks, slots = slot_a.shape
    half = got_a[0].shape[1]
    per = 8
    return pl.pallas_call(
        aggregate_kernel,
        out_shape=jax.ShapeDtypeStruct((2 * half, blocks * TB), jnp.bfloat16),
        grid_spec=pltpu.PrefetchScalarGridSpec(
            num_scalar_prefetch=2,
            grid=(blocks // per,),
            in_specs=[pl.BlockSpec(memory_space=pltpu.HBM)] * (2 * len(LAID))
            + [pl.BlockSpec((per, slots, TB, TB), lambda i, a, b: (i, 0, 0, 0))],
            out_specs=pl.BlockSpec((2 * half, per * TB), lambda i, a, b: (0, i)),
            scratch_shapes=[pltpu.VMEM((SIDE * PART, half, TB), jnp.bfloat16)] * 2
            + [pltpu.SemaphoreType.DMA((2 * len(LAID),))],
        ),
        compiler_params=pltpu.CompilerParams(vmem_limit_bytes=22 * MIB),
        name="aggregate",
    )(slot_a, slot_b, *in_hbm(*got_a, *got_b, vals))


def spread_kernel(slot_a_ref, slot_b_ref, mix_ref, vals_ref, *refs):
    outs, (a_ref, b_ref) = refs[:6], refs[6:]
    step = pl.program_id(0)
    per, slots = vals_ref.shape[:2]
    half = a_ref.shape[1]

    @pl.when(step == 0)
    def _():
        a_ref[...] = jnp.zeros_like(a_ref)
        b_ref[...] = jnp.zeros_like(b_ref)

    for j in range(per):
        i = step * per + j
        mix = mix_ref[:, j * TB : (j + 1) * TB]
        tiles = jnp.concatenate([vals_ref[j, s] for s in range(slots)], axis=1)
        terms = jnp.dot(mix, tiles, preferred_element_type=jnp.float32)
        for s in range(slots):
            term = terms[:, s * TB : (s + 1) * TB]
            a_ref[slot_a_ref[i, s]] += term[:half]
            b_ref[slot_b_ref[i, s]] += term[half:]

    @pl.when(step == pl.num_programs(0) - 1)
    def _():
        for j, held in enumerate((a_ref, b_ref)):
            own, plus, minus = outs[3 * j : 3 * j + 3]
            for out, to, (at, size) in zip((own, plus, minus, plus, minus), (0, 0, 0, PART, PART), LAID):
                out[pl.ds(to, size)] = held[pl.ds(at, size)].astype(jnp.bfloat16)


def spread(slot_a, slot_b, mix, vals):
    blocks, slots = slot_a.shape
    half = mix.shape[0] // 2
    per = 8
    out = pl.pallas_call(
        spread_kernel,
        out_shape=[jax.ShapeDtypeStruct((n, half, TB), jnp.bfloat16) for n in (PART, PART * 3 // 2, PART * 3 // 2) * 2],
        grid_spec=pltpu.PrefetchScalarGridSpec(
            num_scalar_prefetch=2,
            grid=(blocks // per,),
            in_specs=[
                pl.BlockSpec((2 * half, per * TB), lambda i, a, b: (0, i)),
                pl.BlockSpec((per, slots, TB, TB), lambda i, a, b: (i, 0, 0, 0)),
            ],
            out_specs=[
                pl.BlockSpec((n, half, TB), lambda i, a, b: (0, 0, 0), pipeline_mode=pl.Buffered(1))
                for n in (PART, PART * 3 // 2, PART * 3 // 2) * 2
            ],
            scratch_shapes=[pltpu.VMEM((SIDE * PART, half, TB), jnp.float32)] * 2,
        ),
        compiler_params=pltpu.CompilerParams(vmem_limit_bytes=40 * MIB),
        name="spread",
    )(slot_a, slot_b, mix, *in_hbm(vals))
    return out[:3], out[3:]


def fold_kernel(asked_ref, *refs):
    n = len(LAID)
    got, outs, (acc_ref,) = refs[: 2 * n], refs[2 * n : -1], refs[-1:]
    p = pl.program_id(0)
    for h in range(2):
        acc_ref[...] = jnp.zeros_like(acc_ref)

        def add(held, far):
            for start in range(CAP - BATCH, -1, -BATCH):
                at = [
                    pl.ds(pl.multiple_of(asked_ref[h, far, p, k] * TB, TB), TB) for k in range(start, start + BATCH)
                ]
                sums = [acc_ref[:, to] + held[start + j].astype(jnp.float32) for j, to in enumerate(at)]
                for to, total in reversed(list(zip(at, sums))):
                    acc_ref[:, to] = total

        own, plus, minus, upper, lower = got[h * n : h * n + n]
        for held, far in ((own, 0), (plus, 1), (minus, 3)):
            add(held, far)
        pl.when(p < NEAR // 2)(functools.partial(add, upper, 2))
        pl.when(p >= NEAR // 2)(functools.partial(add, lower, 2))
        for plane in range(PLANES):
            for near in range(SIDE):

                @pl.when(p == near * PLANES + plane)
                def _():
                    out = outs[(h * PLANES + plane) * SIDE + near]
                    out[...] = acc_ref[...].astype(out.dtype)


def fold(asked, got, width):
    half = got[0].shape[1]
    block = (CAP, half, TB)
    specs = [pl.BlockSpec(block, lambda p, a: (p, 0, 0))] * 3 + [
        pl.BlockSpec(block, lambda p, a: (jnp.minimum(p, NEAR // 2 - 1), 0, 0)),
        pl.BlockSpec(block, lambda p, a: (jnp.maximum(p - NEAR // 2, 0), 0, 0)),
    ]
    out = pl.pallas_call(
        fold_kernel,
        out_shape=([jax.ShapeDtypeStruct((half, width), jnp.float32)]
            + [jax.ShapeDtypeStruct((half, width), jnp.bfloat16)] * (SIDE - 1))
        * (2 * PLANES),
        grid_spec=pltpu.PrefetchScalarGridSpec(
            num_scalar_prefetch=1,
            grid=(NEAR,),
            in_specs=specs * 2,
            out_specs=[pl.BlockSpec((half, width), lambda p, a: (0, 0), pipeline_mode=pl.Buffered(1))] * (2 * NEAR),
            scratch_shapes=[pltpu.VMEM((half, width), jnp.float32)],
        ),
        compiler_params=pltpu.CompilerParams(vmem_limit_bytes=14 * MIB),
        name="fold",
    )(asked, *got)
    return [[out[(h * PLANES + plane) * SIDE :][:SIDE] for plane in range(PLANES)] for h in range(2)]


def line_sum(folded, plane):
    came = {(h, near): shift(folded[h][plane][near], h, near, 0) for near in (2, 1, 3) for h in range(2)}
    sums = []
    for h in range(2):
        total = folded[h][plane][0]
        for near in range(1, SIDE):
            total = total + came[h, near].astype(jnp.float32)
        sums.append(total)
    return jnp.concatenate(sums, axis=0)


def requests(cols, owners, blocks):
    flat = cols.reshape(-1)
    hit = flat[:, None] == jnp.arange(owners * blocks, dtype=jnp.int32)[None, :]
    named = jnp.any(hit, axis=0).reshape(owners, blocks)
    before = jnp.arange(blocks)[:, None] < jnp.arange(blocks)[None, :]
    rank = jnp.sum(jnp.where(named[:, :, None] & before[None], 1, 0), axis=1).astype(jnp.int32)
    at = named[:, None, :] & (rank[:, None, :] == jnp.arange(CAP, dtype=jnp.int32)[None, :, None])
    wanted = jnp.sum(jnp.where(at, jnp.arange(blocks, dtype=jnp.int32)[None, None, :], 0), axis=2)
    place = jnp.sum(jnp.where(hit, rank.reshape(1, -1), 0), axis=1).astype(jnp.int32)
    return wanted.astype(jnp.int32), place.reshape(cols.shape)


def relative(table, x, y, z):
    for axis, (mine, size) in enumerate(((x, SIDE), (y, SIDE), (z, PLANES))):
        doubled = jnp.concatenate([table, table], axis=axis)
        table = lax.dynamic_slice_in_dim(doubled, mine, size, axis=axis)
    return table


def from_feat(v, step):
    return lax.ppermute(v, "feat", [(i, i ^ step) for i in range(4)])


def every_feat(v):
    two = from_feat(v, 2)
    return v, from_feat(v, 1), two, from_feat(two, 1)


def row_swap(v, dx, dy, dz):
    pairs = [
        ((x * SIDE + y) * PLANES + z, ((x ^ dx) * SIDE + (y ^ dy)) * PLANES + (z ^ dz))
        for x in range(SIDE)
        for y in range(SIDE)
        for z in range(PLANES)
    ]
    return v + lax.ppermute(v, "rows", pairs)


def blocks_by_feat(v, mine):
    size = v.shape[0] // 4
    return jnp.concatenate([lax.dynamic_slice_in_dim(v, (mine ^ j) * size, size, axis=0) for j in range(4)], axis=0)


def on_device(node_feats, tile_vals, tile_cols, weight, bias_vec, grad_out):
    feat_loc, width = node_feats.shape
    own_blocks = tile_cols.shape[0]
    half = feat_loc // 2
    me = lax.axis_index("rows")
    x, y, z = me // NEAR, (me // PLANES) % SIDE, me % PLANES
    mine = lax.axis_index("feat")

    other = lax.ppermute(node_feats, "rows", row_perm(0, 0, 1))
    wanted, place = requests(tile_cols, SIDE * NEAR, own_blocks)
    owner = tile_cols // own_blocks
    dx, dy = (owner // NEAR - x) % SIDE, ((owner // PLANES) % SIDE - y) % SIDE
    dz = (owner - z) % PLANES
    slots = [
        ((far * SIDE + near) * PLANES + dz) * CAP + place for near, far in ((dx, dy), (dy, dx))
    ]
    by_place = relative(wanted.reshape(SIDE, SIDE, PLANES, CAP), x, y, z)
    tables = [by_place.transpose(1, 0, 2, 3).reshape(SIDE, NEAR, CAP), by_place.reshape(SIDE, NEAR, CAP)]
    shards = []
    for h in range(2):
        rows = slice(h * half, (h + 1) * half)
        aside = jnp.pad(tables[1 - h].reshape(SIDE, PART).astype(jnp.bfloat16), ((0, feat_loc - SIDE), (0, 0)))
        both = jnp.concatenate([node_feats[rows], other[rows]], axis=0)
        shards.append(jnp.concatenate([both, aside], axis=1))
    first = [[shift(shards[h], h, -1, 0), shift(shards[h], h, 1, 0)] for h in range(2)]
    second = [[shift(first[h][0][:half], h, -1, 0), shift(first[h][1][half:], h, 1, 0)] for h in range(2)]
    lines = [v for h in range(2) for v in (shards[h], *first[h], *second[h])]
    asked = []
    for h in range(2):
        (plus, minus), (upper, _) = first[1 - h], second[1 - h]
        heard = [v[far, width:].astype(jnp.int32) for far, v in ((1, minus), (2, upper), (3, plus))]
        asked.append(jnp.stack([tables[h][0]] + [v.reshape(NEAR, CAP) for v in heard]))
    asked = jnp.stack(asked)
    lines, weight, bias_vec, grad_out = lax.optimization_barrier((lines, weight, bias_vec, grad_out))

    wide = jnp.concatenate([weight.astype(jnp.float32), jnp.broadcast_to(bias_vec[None], (8, feat_loc))], axis=0)
    wide = jnp.concatenate(every_feat(wide), axis=1)
    weight_all = blocks_by_feat(wide[: weight.shape[0]].astype(jnp.bfloat16), mine)
    bias_all = wide[weight.shape[0]]
    grad_out_all = jnp.concatenate(every_feat(grad_out), axis=0)

    got, _ = exchange(pack(asked, lines), -1)
    aggregated = aggregate(*slots, *got, tile_vals)
    agg_all = jnp.concatenate(every_feat(aggregated), axis=0)
    preact = (
        lax.dot_general(weight_all, agg_all, (((0,), (0,)), ((), ())), preferred_element_type=jnp.float32)
        + bias_all[:, None]
    )
    sigma = jax.nn.sigmoid(preact)
    activated = (preact[:feat_loc] * sigma[:feat_loc]).astype(jnp.bfloat16)
    grad_pre = (grad_out_all.astype(jnp.float32) * sigma * (1.0 + preact * (1.0 - sigma))).astype(jnp.bfloat16)
    back_mix = jnp.dot(weight_all[:feat_loc], grad_pre, preferred_element_type=jnp.float32).astype(jnp.bfloat16)

    terms = spread(*slots, back_mix, tile_vals)
    own_grad = grad_pre[:feat_loc]
    weight_part = lax.dot_general(own_grad, agg_all, (((1,), (1,)), ((), ())), preferred_element_type=jnp.float32)
    bias_part = jnp.sum(own_grad.astype(jnp.float32), axis=1)
    bias_rows = jnp.broadcast_to(jnp.pad(bias_part, (0, weight.shape[0] - feat_loc))[None], (8, weight.shape[0]))
    parts = jnp.concatenate([weight_part, bias_rows], axis=0)
    parts = row_swap(row_swap(parts, 0, 0, 1), 0, 1, 0)

    back, parts = exchange(terms, 1, parts)
    parts = row_swap(parts, 0, 2, 0)
    back, parts = lax.optimization_barrier((back, parts))
    folded = fold(asked, back[0] + back[1], width)
    passed, parts = line_sum(folded, 1).astype(jnp.bfloat16), parts
    passed, folded, parts = lax.optimization_barrier((passed, folded, parts))
    arrived = lax.ppermute(passed, "rows", row_perm(0, 0, 1))
    grad_feats = line_sum(folded, 0) + arrived.astype(jnp.float32)
    parts = row_swap(row_swap(parts, 1, 0, 0), 2, 0, 0)
    grad_bias = parts[feat_loc, :feat_loc]
    grad_weight = blocks_by_feat(parts[:feat_loc].T, mine)
    return (activated, grad_feats, grad_weight, grad_bias)


def solution(mesh):
    placed = (
        P("feat", "rows"),
        P("rows", None, None, None),
        P("rows", None),
        P(None, "feat"),
        P("feat"),
        P("feat", "rows"),
    )
    return jax.shard_map(
        on_device,
        mesh=mesh,
        in_specs=placed,
        out_specs=(P("feat", "rows"), P("feat", "rows"), P(None, "feat"), P("feat")),
        check_vma=False,
    )
```
